32 devices in a mesh: section: 4 (over z), vit: 2 (over x), dp: 4 (over y, core).
Axes of the slice: x: 2, y: 2, z: 4, core: 2. Of those that a mesh axis runs over, the one named last changes fastest.
Arguments:
- grad_llm: bfloat16 [4, 1024, 4096], P('section', ('dp', 'vit')), parts along dimension 1, may hold values from -6 to 6
- vis_slot: int32 [8, 128], P('dp'), parts along dimension 0, may hold values from 0 to 255, as said below
- image_rows: int32 [16, 2], P('dp'), parts along dimension 0, may hold values from 8 to 32, as said below
- section_layer: int32 [4], replicated, may hold values from 0 to 3, each once
- vit_in: bfloat16 [4096, 1152], P(('dp', 'section', 'vit')), parts along dimension 0, may hold values from -6 to 6
- vit_out: bfloat16 [4096, 1152], P(('dp', 'section', 'vit')), parts along dimension 0, may hold values from -6 to 6
- ln_gain: float32 [1152], replicated, may hold values from 0.5 to 1.5
- ln_bias: float32 [1152], replicated, may hold values from -3 to 3
- qkv_weight: bfloat16 [1152, 3456], P('section'), may hold values from -0.1875 to 0.1875
- proj_weight: bfloat16 [1152, 1152], P('section'), may hold values from -0.1875 to 0.1875
- merge_gain: float32 [1152], replicated, may hold values from 0.5 to 1.5
- merge_bias: float32 [1152], replicated, may hold values from -3 to 3
- fc1_weight: bfloat16 [4608, 4608], P(None, 'vit'), may hold values from -0.09375 to 0.09375
- fc1_bias: float32 [4608], P('vit'), may hold values from -3 to 3
- fc2_weight: bfloat16 [4608, 4096], P('vit'), may hold values from -0.09375 to 0.09375
Outputs:
- vit_grad: bfloat16 [4096, 1152], P(('dp', 'section', 'vit')), parts along dimension 0
The draws below stay inside these ranges and needn't reach their ends.
There are 4 independent parts, one for each index of `dp`. The reference program is written for one: setup_inputs(seed, part) draws one part's arguments, and reference() takes and returns one part's arrays. A program takes and returns all parts, laid end to end along the dimension named above; an argument that names none is the same for every part. Nothing has to cross between parts.
Inputs may be any that keep to these rules, and one draw needn't show every extreme that they name: `vis_slot`: every slot number appears once. On every language-model device v, the rows d * 16 to d * 16 + 15 name 16 consecutive slots that start at a multiple of 16 inside d * 32 to d * 32 + 31, the slots of vision device d (devices numbered with the group first). `image_rows`: in every group one image has exactly 32 merged tokens. `section_layer`: A permutation; the section with value 3 holds no DeepStack layer.
All inputs are finite; a program needn't handle non-finite values.
Results may differ from the reference program's by a relative error of at most 0.02.
Values may be sent and summed in bfloat16 or wider, within the bound.
No kernel may reach another device: no remote copies, remote signals or barrier semaphores. Data moves between devices by JAX's collectives and lax.ppermute only.
A program may use at most 128 MiB of HBM per device.

```python
import jax
import jax.numpy as jnp
from jax import lax

DV = 1152
HEADS = 16
DL = 4096
LEVELS = 3
SLOTS = 32
HD = 72
DM = 4608
RUN = 16
LLM_ROWS = 128
IMAGES = 2
GROUP_SLOTS = 64
N_SECTION = 4
N_VIT = 2


def draw_vis_slot(key, part):
    devices = N_SECTION * N_VIT
    device_keys = jax.random.split(jax.random.fold_in(key, 11), devices)
    orders = jax.vmap(jax.random.permutation, in_axes=(0, None))(device_keys, N_VIT).astype(jnp.int32)
    device_id = jnp.arange(devices, dtype=jnp.int32)
    within = jnp.arange(RUN, dtype=jnp.int32)
    slots = device_id[None, :, None] * SLOTS + RUN * orders.T[:, :, None] + within[None, None, :]
    return slots.reshape(N_VIT, LLM_ROWS).astype(jnp.int32)


def draw_image_rows(key, part):
    counts = jax.random.randint(jax.random.fold_in(key, 3), (N_SECTION, IMAGES), SLOTS // 4, SLOTS + 1)
    chosen = jax.random.randint(jax.random.fold_in(key, 5), (N_SECTION, 1), 0, IMAGES)
    column = jnp.arange(IMAGES, dtype=jnp.int32)[None, :]
    return jnp.where(column == chosen, SLOTS, counts).astype(jnp.int32)


def levels(rng, dims, shards, smallest, top_value):
    level, own = 1.0, jax.random.fold_in(rng, 6)
    for dim, parts in shards:
        draws = jnp.exp(jax.random.uniform(jax.random.fold_in(own, dim), (parts,), jnp.float32, smallest / len(shards), top_value / len(shards)))
        level = level * jnp.repeat(draws, dims[dim] // parts).reshape([-1 if axis == dim else 1 for axis in range(len(dims))])
    return level


def centred(rng, extent, deviation, reach, pieces=(), kind=jnp.bfloat16):
    level = levels(rng, extent, pieces, -0.22, 0.18) if pieces else 1.0
    values = jax.random.normal(rng, extent, jnp.float32) * deviation * level
    return jnp.minimum(jnp.maximum(values, -reach), reach).astype(kind)


def setup_inputs(seed: int = 0, part: int = 0) -> dict:
    streams_of = jax.random.split(jax.random.key(seed), 16)
    own_keys = jax.random.split(jax.random.fold_in(streams_of[15], part), 16)
    return {
        "grad_llm": centred(own_keys[0], (N_SECTION, N_VIT * LLM_ROWS, DL), 1.0, 6.0, ((0, 4), (1, 2))),
        "vis_slot": draw_vis_slot(jax.random.fold_in(jax.random.fold_in(streams_of[15], part), 71), part),
        "image_rows": draw_image_rows(jax.random.fold_in(jax.random.fold_in(streams_of[15], part), 71), part),
        "section_layer": jax.random.permutation(streams_of[3], N_SECTION).astype(jnp.int32),
        "vit_in": centred(own_keys[4], (N_SECTION * GROUP_SLOTS * 4, DV), 1.0, 6.0, ((0, 8),)),
        "vit_out": centred(own_keys[5], (N_SECTION * GROUP_SLOTS * 4, DV), 1.0, 6.0, ((0, 8),)),
        "ln_gain": jnp.clip(1.0 + 0.1 * jax.random.normal(streams_of[6], (DV,), jnp.float32), 0.5, 1.5),
        "ln_bias": centred(streams_of[7], (DV,), 0.5, 3.0, (), jnp.float32),
        "qkv_weight": centred(streams_of[8], (DV, 3 * DV), DV ** -0.5, 0.1875, ((0, 4),)),
        "proj_weight": centred(streams_of[9], (DV, DV), DV ** -0.5, 0.1875, ((0, 4),)),
        "merge_gain": jnp.clip(1.0 + 0.1 * jax.random.normal(streams_of[10], (DV,), jnp.float32), 0.5, 1.5),
        "merge_bias": centred(streams_of[11], (DV,), 0.5, 3.0, (), jnp.float32),
        "fc1_weight": centred(streams_of[12], (DM, DM), DM ** -0.5, 0.09375, ((1, 2),)),
        "fc1_bias": centred(streams_of[13], (DM,), 0.5, 3.0, ((0, 2),), jnp.float32),
        "fc2_weight": centred(streams_of[14], (DM, DL), DM ** -0.5, 0.09375, ((0, 2),)),
    }


norm_eps = 1e-06

def normalize(values):
    row_mean = lax.optimization_barrier(jnp.mean(values, axis=-1, keepdims=True))
    centered = values - row_mean
    variance = lax.optimization_barrier(jnp.mean(centered * centered, axis=-1, keepdims=True))
    inverse = lax.rsqrt(variance + norm_eps)
    return (centered * inverse, inverse)

def normalize_back(upstream, normed_rows, inverse, gain):
    scaled = upstream * gain
    mean_scaled = lax.optimization_barrier(jnp.mean(scaled, axis=-1, keepdims=True))
    mean_cross = lax.optimization_barrier(jnp.mean(scaled * normed_rows, axis=-1, keepdims=True))
    return (scaled - mean_scaled - normed_rows * mean_cross) * inverse

def gelu_slope(pre_act):
    cumulative = 0.5 * (1.0 + lax.erf(pre_act * 0.7071067811865476))
    density = jnp.exp(-0.5 * pre_act * pre_act) * 0.3989422804014327
    return cumulative + pre_act * density

def slot_layout(image_rows):
    image_ends = jnp.cumsum(image_rows, axis=1).astype(jnp.int32)
    position = jnp.arange(GROUP_SLOTS, dtype=jnp.int32)
    slot_image = lax.optimization_barrier(jnp.sum((position[None, :, None] >= image_ends[:, None, :]).astype(jnp.int32), axis=2))
    slot_live = position[None, :] < image_ends[:, -1:]
    return (slot_image, slot_live)

def reference(grad_llm, vis_slot, image_rows, section_layer, vit_in, vit_out, ln_gain, ln_bias, qkv_weight, proj_weight, merge_gain, merge_bias, fc1_weight, fc1_bias, fc2_weight):
    all_slots = N_SECTION * GROUP_SLOTS
    section_weight = jnp.where(section_layer < LEVELS, (section_layer + 1).astype(jnp.float32) / LEVELS, 0.0).astype(jnp.float32)
    summed = jnp.zeros((N_VIT * LLM_ROWS, DL), jnp.float32)
    for section_index in range(N_SECTION):
        summed = summed + section_weight[section_index] * grad_llm[section_index].astype(jnp.float32)
    placed = jnp.zeros((all_slots, DL), jnp.float32).at[vis_slot.reshape(-1)].set(summed)
    slot_image, slot_live = slot_layout(image_rows)
    merged_grad = jnp.where(slot_live.reshape(-1)[:, None], placed, 0.0).astype(jnp.bfloat16)
    out_rows, out_inverse = normalize(vit_out.astype(jnp.float32))
    merge_in = (out_rows * merge_gain + merge_bias).astype(jnp.bfloat16).reshape(all_slots, DM)
    pre_act = jnp.dot(merge_in, fc1_weight, preferred_element_type=jnp.float32) + fc1_bias
    hidden_grad = jnp.dot(merged_grad, fc2_weight.T, preferred_element_type=jnp.float32)
    pre_grad = (hidden_grad * gelu_slope(pre_act)).astype(jnp.bfloat16)
    block_width = DM // N_VIT
    merge_grad = jnp.zeros((all_slots, DM), jnp.float32)
    for block_index in range(N_VIT):
        first = block_index * block_width
        block_term = jnp.dot(pre_grad[:, first:first + block_width], fc1_weight[:, first:first + block_width].T, preferred_element_type=jnp.float32)
        rounded = lax.optimization_barrier(block_term.astype(jnp.bfloat16))
        merge_grad = merge_grad + rounded.astype(jnp.float32)
    out_grad = normalize_back(merge_grad.reshape(-1, DV), out_rows, out_inverse, merge_gain).astype(jnp.bfloat16)
    in_rows, in_inverse = normalize(vit_in.astype(jnp.float32))
    normed = (in_rows * ln_gain + ln_bias).astype(jnp.bfloat16)
    projected = jnp.dot(normed, qkv_weight, preferred_element_type=jnp.float32).astype(jnp.bfloat16)
    out_proj_grad = jnp.dot(out_grad, proj_weight.T, preferred_element_type=jnp.float32).astype(jnp.bfloat16)
    length = 4 * GROUP_SLOTS
    per_head = projected.reshape(N_SECTION, length, 3, HEADS, HD).transpose(2, 0, 3, 1, 4).reshape(3, N_SECTION * HEADS, length, HD)
    grad_heads = out_proj_grad.reshape(N_SECTION, length, HEADS, HD).transpose(0, 2, 1, 3).reshape(N_SECTION * HEADS, length, HD)
    patch_image = jnp.repeat(slot_image, 4, axis=1)
    patch_live = jnp.repeat(slot_live, 4, axis=1)
    group_of = (jnp.arange(N_SECTION * HEADS, dtype=jnp.int32) // HEADS).astype(jnp.int32)
    score_scale = HD ** (-0.5)

    def one_head(inputs):
        query_rows, key_rows, value_rows, grad_rows, group_index = inputs
        image_here = lax.dynamic_index_in_dim(patch_image, group_index, 0, keepdims=False)
        live_here = lax.dynamic_index_in_dim(patch_live, group_index, 0, keepdims=False)
        scores = jnp.dot(query_rows, key_rows.T, preferred_element_type=jnp.float32) * score_scale
        allowed = (image_here[:, None] == image_here[None, :]) & live_here[:, None] & live_here[None, :]
        exponent = jnp.where(allowed, jnp.exp(jnp.where(allowed, scores, 0.0)), 0.0)
        denominator = lax.optimization_barrier(jnp.sum(exponent, axis=1, keepdims=True)) + 1.0 - live_here.astype(jnp.float32)[:, None]
        softmax_weights = (exponent / denominator).astype(jnp.bfloat16)
        prob_grad = jnp.dot(grad_rows, value_rows.T, preferred_element_type=jnp.float32)
        weighted = softmax_weights.astype(jnp.float32)
        row_dot = lax.optimization_barrier(jnp.sum(weighted * prob_grad, axis=1, keepdims=True))
        score_grad = (weighted * (prob_grad - row_dot) * score_scale).astype(jnp.bfloat16)
        query_grad = jnp.dot(score_grad, key_rows, preferred_element_type=jnp.float32).astype(jnp.bfloat16)
        key_grad = jnp.dot(score_grad.T, query_rows, preferred_element_type=jnp.float32).astype(jnp.bfloat16)
        value_grad = jnp.dot(softmax_weights.T, grad_rows, preferred_element_type=jnp.float32).astype(jnp.bfloat16)
        return jnp.stack([query_grad, key_grad, value_grad])
    head_grads = lax.map(one_head, (per_head[0], per_head[1], per_head[2], grad_heads, group_of))
    projected_grad = head_grads.reshape(N_SECTION, HEADS, 3, length, HD).transpose(0, 3, 2, 1, 4).reshape(all_slots * 4, 3 * DV)
    normed_grad = jnp.dot(projected_grad, qkv_weight.T, preferred_element_type=jnp.float32)
    vit_grad = (out_grad.astype(jnp.float32) + normalize_back(normed_grad, in_rows, in_inverse, ln_gain)).astype(jnp.bfloat16)
    return vit_grad
```

```python
import jax
import jax.numpy as jnp
from jax import lax
from jax.sharding import PartitionSpec as P

HEADS = 16
LEVELS = 3


norm_eps = 1e-06


def normalize(values):
    row_mean = jnp.mean(values, axis=-1, keepdims=True)
    centered = values - row_mean
    variance = jnp.mean(centered * centered, axis=-1, keepdims=True)
    inverse = lax.rsqrt(variance + norm_eps)
    return (centered * inverse, inverse)


def normalize_back(upstream, normed_rows, inverse, gain):
    scaled = upstream * gain
    mean_scaled = jnp.mean(scaled, axis=-1, keepdims=True)
    mean_cross = jnp.mean(scaled * normed_rows, axis=-1, keepdims=True)
    return (scaled - mean_scaled - normed_rows * mean_cross) * inverse


def gelu_slope(pre_act):
    cumulative = 0.5 * (1.0 + lax.erf(pre_act * 0.7071067811865476))
    density = jnp.exp(-0.5 * pre_act * pre_act) * 0.3989422804014327
    return cumulative + pre_act * density


def local(
    grad_llm,
    vis_slot,
    image_rows,
    section_layer,
    vit_in,
    vit_out,
    ln_gain,
    ln_bias,
    qkv_weight,
    proj_weight,
    merge_gain,
    merge_bias,
    fc1_weight,
    fc1_bias,
    fc2_weight,
):
    sections = lax.axis_size("section")
    shards = lax.axis_size("vit")
    section_index = lax.axis_index("section")
    shard_index = lax.axis_index("vit")
    devices = sections * shards
    patches = vit_in.shape[0]
    slots_here = patches // 4
    run_rows = grad_llm.shape[1] // devices
    llm_width = grad_llm.shape[2]
    vit_width = vit_in.shape[1]
    head_dim = vit_width // HEADS
    device_index = section_index * shards + shard_index
    qkv_full, proj_full = (
        lax.all_gather(qkv_weight, "section", axis=0, tiled=True),
        lax.all_gather(proj_weight, "section", axis=0, tiled=True),
    )
    in_rows, in_inverse = normalize(vit_in.astype(jnp.float32))
    normed = (in_rows * ln_gain + ln_bias).astype(jnp.bfloat16)
    projected = lax.dot_general(
        qkv_full, normed, (((0,), (1,)), ((), ())), preferred_element_type=jnp.float32
    )
    projected = projected.astype(jnp.bfloat16).reshape(3, HEADS, head_dim, patches)
    section_weight = jnp.where(
        section_layer < LEVELS, (section_layer + 1).astype(jnp.float32) / LEVELS, 0.0
    )
    outgoing = grad_llm[0].reshape(devices, run_rows, llm_width)
    image_ends = jnp.cumsum(image_rows[section_index])
    out_rows, out_inverse = normalize(vit_out.astype(jnp.float32))
    merge_in = (
        (out_rows * merge_gain + merge_bias).astype(jnp.bfloat16).reshape(slots_here, 4 * vit_width)
    )
    arrived = lax.all_to_all(outgoing, ("section", "vit"), split_axis=0, concat_axis=0, tiled=True)
    arrived_f = arrived.reshape(sections, shards, run_rows, llm_width).astype(jnp.float32)
    incoming = jnp.sum(arrived_f * section_weight[:, None, None, None], axis=0)
    columns = lax.dynamic_slice_in_dim(vis_slot, device_index * run_rows, run_rows, 1)
    local_slot = (columns - device_index * slots_here).reshape(-1)
    placed = (
        jnp.zeros((slots_here, llm_width), jnp.float32)
        .at[local_slot]
        .set(incoming.reshape(-1, llm_width))
    )
    slot_position = shard_index * slots_here + jnp.arange(slots_here, dtype=jnp.int32)
    merged_grad = jnp.where((slot_position < image_ends[-1])[:, None], placed, 0.0).astype(
        jnp.bfloat16
    )
    rows_in, rows_grad = (
        lax.all_gather(merge_in, "vit", axis=0, tiled=True),
        lax.all_gather(merged_grad, "vit", axis=0, tiled=True),
    )
    pre_act = jnp.dot(rows_in, fc1_weight, preferred_element_type=jnp.float32) + fc1_bias
    hidden_grad = lax.dot_general(
        rows_grad, fc2_weight, (((1,), (1,)), ((), ())), preferred_element_type=jnp.float32
    )
    pre_grad = (hidden_grad * gelu_slope(pre_act)).astype(jnp.bfloat16)
    merge_grad = lax.psum_scatter(
        lax.dot_general(
            pre_grad, fc1_weight, (((1,), (1,)), ((), ())), preferred_element_type=jnp.float32
        ).astype(jnp.bfloat16),
        "vit",
        scatter_dimension=0,
        tiled=True,
    ).astype(jnp.float32)
    out_grad = normalize_back(
        merge_grad.reshape(patches, vit_width), out_rows, out_inverse, merge_gain
    ).astype(jnp.bfloat16)
    grad_cols = lax.dot_general(
        proj_full, out_grad, (((1,), (1,)), ((), ())), preferred_element_type=jnp.float32
    )
    grad_cols = grad_cols.astype(jnp.bfloat16).reshape(1, HEADS, head_dim, patches)
    head_inputs, head_grad = (
        lax.all_to_all(projected, "vit", split_axis=1, concat_axis=3, tiled=True),
        lax.all_to_all(grad_cols, "vit", split_axis=1, concat_axis=3, tiled=True),
    )
    length = shards * patches
    block_size = min(512, length)
    block_count = length // block_size
    slot_of = jnp.arange(length, dtype=jnp.int32) // 4
    patch_image = jnp.sum((slot_of[:, None] >= image_ends[None, :]).astype(jnp.int32), axis=1)
    patch_live = slot_of < image_ends[-1]
    score_scale = head_dim ** (-0.5)
    contract_first = (((0,), (0,)), ((), ()))

    def head_backward(query_cols, key_cols, value_cols, grad_head):

        def step(carry, block_index):
            key_acc, value_acc = carry
            first_row = block_index * block_size
            query_block = lax.dynamic_slice_in_dim(query_cols, first_row, block_size, 1)
            grad_block = lax.dynamic_slice_in_dim(grad_head, first_row, block_size, 1)
            image_block = lax.dynamic_slice_in_dim(patch_image, first_row, block_size, 0)
            live_block = lax.dynamic_slice_in_dim(patch_live, first_row, block_size, 0)
            scores = (
                lax.dot_general(
                    query_block, key_cols, contract_first, preferred_element_type=jnp.float32
                )
                * score_scale
            )
            allowed = (
                (image_block[:, None] == patch_image[None, :])
                & live_block[:, None]
                & patch_live[None, :]
            )
            exponent = jnp.where(allowed, jnp.exp(jnp.where(allowed, scores, 0.0)), 0.0)
            denominator = (
                jnp.sum(exponent, axis=1, keepdims=True)
                + 1.0
                - live_block.astype(jnp.float32)[:, None]
            )
            softmax_weights = (exponent / denominator).astype(jnp.bfloat16)
            prob_grad = lax.dot_general(
                grad_block, value_cols, contract_first, preferred_element_type=jnp.float32
            )
            weighted = softmax_weights.astype(jnp.float32)
            row_dot = jnp.sum(weighted * prob_grad, axis=1, keepdims=True)
            score_grad = (weighted * (prob_grad - row_dot) * score_scale).astype(jnp.bfloat16)
            query_grad = lax.dot_general(
                key_cols, score_grad, (((1,), (1,)), ((), ())), preferred_element_type=jnp.float32
            )
            key_acc = key_acc + lax.dot_general(
                query_block,
                score_grad,
                (((1,), (0,)), ((), ())),
                preferred_element_type=jnp.float32,
            )
            value_acc = value_acc + lax.dot_general(
                grad_block,
                softmax_weights,
                (((1,), (0,)), ((), ())),
                preferred_element_type=jnp.float32,
            )
            return ((key_acc, value_acc), query_grad.astype(jnp.bfloat16))

        empty = jnp.zeros((head_dim, length), jnp.float32)
        (key_total, value_total), query_blocks = lax.scan(
            step, (empty, empty), jnp.arange(block_count, dtype=jnp.int32)
        )
        query_total = query_blocks.transpose(1, 0, 2).reshape(head_dim, length)
        return (query_total, key_total.astype(jnp.bfloat16), value_total.astype(jnp.bfloat16))

    query_all, key_all, value_all = jax.vmap(head_backward)(
        head_inputs[0], head_inputs[1], head_inputs[2], head_grad[0]
    )
    head_result = jnp.stack([query_all, key_all, value_all])
    returned = lax.all_to_all(head_result, "vit", split_axis=3, concat_axis=1, tiled=True)
    projected_grad = returned.reshape(3 * vit_width, patches)
    normed_grad = lax.dot_general(
        projected_grad, qkv_full, (((0,), (1,)), ((), ())), preferred_element_type=jnp.float32
    )
    vit_grad = out_grad.astype(jnp.float32) + normalize_back(
        normed_grad, in_rows, in_inverse, ln_gain
    )
    return vit_grad.astype(jnp.bfloat16)


def swap(values, axis, bit):
    count = lax.axis_size(axis)
    return lax.ppermute(values, axis, [(i, i ^ bit) for i in range(count)])


def fits(mesh, heads, head_dim, part_rows):
    sections, copies, shards = (mesh.shape[name] for name in ("section", "dp", "vit"))
    if (sections, copies, shards) != (4, 4, 2) or heads % (shards * copies):
        return False
    return part_rows % (heads // (shards * copies) * head_dim) == 0


def local_paired(
    grad_llm,
    vis_slot,
    image_rows,
    section_layer,
    vit_in,
    vit_out,
    ln_gain,
    ln_bias,
    qkv_weight,
    proj_weight,
    merge_gain,
    merge_bias,
    fc1_weight,
    fc1_bias,
    fc2_weight,
):
    sections = lax.axis_size("section")
    shards = lax.axis_size("vit")
    copies = lax.axis_size("dp")
    section_index = lax.axis_index("section")
    shard_index = lax.axis_index("vit")
    copy_index = lax.axis_index("dp")
    patches = vit_in.shape[0]
    slots_here = patches // 4
    llm_width = grad_llm.shape[2]
    vit_width = vit_in.shape[1]
    head_dim = vit_width // HEADS
    part_rows = qkv_weight.shape[0]
    group_heads = HEADS // (shards * copies)
    group_cols = group_heads * head_dim
    group_rows = grad_llm.shape[1] // sections
    length = shards * patches
    bf16, f32 = jnp.bfloat16, jnp.float32

    outgoing = grad_llm[0].reshape(sections, group_rows, llm_width)

    def for_section(k):
        return lax.dynamic_index_in_dim(outgoing, section_index ^ k, 0, keepdims=False)

    arrived = [for_section(0)] + [swap(for_section(k), "section", k) for k in range(1, sections)]
    vit_out_all = jnp.concatenate([vit_out, swap(vit_out, "vit", 1)], axis=0)
    vit_in_all = jnp.concatenate([vit_in, swap(vit_in, "vit", 1)], axis=0)

    heads_of = qkv_weight.reshape(part_rows, 3, HEADS, head_dim)

    def own_group(p):
        first = (shard_index * copies + (copy_index ^ p)) * group_heads
        return lax.dynamic_slice_in_dim(heads_of, first, group_heads, 2).reshape(part_rows, -1)

    def spread(piece):
        other_chip = swap(piece, "dp", 2)
        return [piece, swap(piece, "dp", 1), other_chip, swap(other_chip, "dp", 1)]

    piece = own_group(0)
    near = swap(piece, "section", 1)
    far = swap(piece, "section", 2)
    cross = swap(far, "section", 1)
    qkv_parts = [[own_group(p) for p in range(copies)]] + [spread(x) for x in (near, far, cross)]
    qkv_groups = jnp.concatenate(
        [jnp.concatenate(parts, axis=1) for parts in qkv_parts], axis=0
    )

    def source_of(v, q):
        return (v * copies + q) * group_cols // part_rows

    def hop(values, first, second):
        pairs = []
        for v in range(shards):
            for q in range(copies):
                t = source_of(v, q)
                flat = [((t ^ b) * shards + v) * copies + q for b in (first, second)]
                pairs.append(tuple(flat))
        return lax.ppermute(values, ("section", "vit", "dp"), pairs)

    first_row = (shard_index * copies + copy_index) * group_cols
    proj_own = lax.dynamic_slice_in_dim(proj_weight, first_row % part_rows, group_cols, 0)
    relation = section_index ^ (first_row // part_rows)
    proj_near = hop(proj_own, 0, 1)
    proj_far = hop(proj_own, 0, 2)
    proj_cross = hop(proj_far, 2, 3)
    proj_piece = jnp.where(
        relation == 0,
        proj_own,
        jnp.where(relation == 1, proj_near, jnp.where(relation == 2, proj_far, proj_cross)),
    )
    proj_groups = jnp.concatenate(spread(proj_piece), axis=0)

    in_rows, in_inverse = normalize(vit_in_all.astype(f32))
    normed = (in_rows * ln_gain + ln_bias).astype(bf16)

    def part_cols(values, k):
        return lax.dynamic_slice_in_dim(values, (section_index ^ k) * part_rows, part_rows, 1)

    normed_parts = jnp.concatenate([part_cols(normed, k) for k in range(sections)], axis=1)
    projected = jnp.dot(normed_parts, qkv_groups, preferred_element_type=f32).astype(bf16)
    out_rows, out_inverse = normalize(vit_out_all.astype(f32))
    merge_in = (out_rows * merge_gain + merge_bias).astype(bf16).reshape(-1, 4 * vit_width)

    section_weight = jnp.where(
        section_layer < LEVELS, (section_layer + 1).astype(f32) / LEVELS, 0.0
    )
    summed = sum(
        section_weight[section_index ^ k] * arrived[k].astype(f32) for k in range(sections)
    ).astype(bf16)
    rows_grad = jnp.concatenate([summed, swap(summed, "vit", 1)], axis=0)
    image_ends = jnp.cumsum(image_rows[section_index])
    halves = jnp.arange(shards, dtype=jnp.int32) ^ shard_index
    slot_position = (
        halves[:, None] * slots_here + jnp.arange(slots_here, dtype=jnp.int32)
    ).reshape(-1)
    named = lax.dynamic_slice_in_dim(vis_slot, section_index * group_rows, group_rows, 1)
    named = jnp.where(shard_index == 0, named, named[::-1]).reshape(-1)
    named = named - section_index * shards * slots_here
    chosen = (slot_position[:, None] == named[None, :]) & (slot_position < image_ends[-1])[:, None]
    merged_grad = jnp.dot(chosen.astype(bf16), rows_grad, preferred_element_type=f32).astype(bf16)

    pre_act = jnp.dot(merge_in, fc1_weight, preferred_element_type=f32) + fc1_bias
    hidden_grad = lax.dot_general(
        merged_grad, fc2_weight, (((1,), (1,)), ((), ())), preferred_element_type=f32
    )
    pre_grad = (hidden_grad * gelu_slope(pre_act)).astype(bf16)
    partial = lax.dot_general(
        pre_grad, fc1_weight, (((1,), (1,)), ((), ())), preferred_element_type=f32
    ).astype(bf16)
    theirs = swap(partial, "vit", 1)
    theirs = jnp.concatenate([theirs[slots_here:], theirs[:slots_here]], axis=0)
    merge_grad = partial.astype(f32) + theirs.astype(f32)
    out_grad = normalize_back(
        merge_grad.reshape(length, vit_width), out_rows, out_inverse, merge_gain
    ).astype(bf16)
    grad_cols = lax.dot_general(
        out_grad, proj_groups, (((1,), (1,)), ((), ())), preferred_element_type=f32
    ).astype(bf16)

    patch_slot = jnp.repeat(slot_position, 4)
    patch_image = jnp.sum((patch_slot[:, None] >= image_ends[None, :]).astype(jnp.int32), axis=1)
    patch_live = patch_slot < image_ends[-1]
    score_scale = head_dim ** (-0.5)
    allowed = (
        (patch_image[:, None] == patch_image[None, :]) & patch_live[:, None] & patch_live[None, :]
    )
    heads_here = HEADS // shards
    split = projected.reshape(length, copies, 3, group_heads, head_dim).transpose(2, 1, 3, 0, 4)
    split = split.reshape(3, heads_here, length, head_dim)
    query, key, value = split[0], split[1], split[2]
    grad_heads = grad_cols.reshape(length, heads_here, head_dim).transpose(1, 0, 2)

    def pair(a, b, ca, cb):
        return lax.dot_general(a, b, (((ca,), (cb,)), ((0,), (0,))), preferred_element_type=f32)

    scores = pair(query, key, 2, 2) * score_scale
    exponent = jnp.where(allowed, jnp.exp(jnp.where(allowed, scores, 0.0)), 0.0)
    denominator = (
        jnp.sum(exponent, axis=2, keepdims=True) + 1.0 - patch_live.astype(f32)[None, :, None]
    )
    softmax_weights = (exponent / denominator).astype(bf16)
    prob_grad = pair(grad_heads, value, 2, 2)
    weighted = softmax_weights.astype(f32)
    row_dot = jnp.sum(weighted * prob_grad, axis=2, keepdims=True)
    score_grad = (weighted * (prob_grad - row_dot) * score_scale).astype(bf16)
    query_grad = pair(score_grad, key, 2, 1)
    key_grad = pair(score_grad, query, 1, 1)
    value_grad = pair(softmax_weights, grad_heads, 1, 1)
    projected_grad = (
        jnp.stack([query_grad, key_grad, value_grad])
        .astype(bf16)
        .reshape(3, copies, group_heads, length, head_dim)
        .transpose(3, 1, 0, 2, 4)
        .reshape(length, -1)
    )

    normed_grad = lax.dot_general(
        projected_grad, qkv_groups, (((1,), (1,)), ((), ())), preferred_element_type=f32
    )
    theirs = swap(normed_grad[patches:].astype(bf16), "vit", 1)
    normed_grad = normed_grad[:patches] + theirs.astype(f32)
    normed_grad = jnp.concatenate([part_cols(normed_grad, k) for k in range(sections)], axis=1)
    vit_grad = out_grad[:patches].astype(f32) + normalize_back(
        normed_grad, in_rows[:patches], in_inverse[:patches], ln_gain
    )
    return vit_grad.astype(bf16)


def solution(mesh):
    def chosen_form(*arguments):
        width, part_rows = arguments[4].shape[1], arguments[8].shape[0]
        paired = fits(mesh, HEADS, width // HEADS, part_rows)
        return (local_paired if paired else local)(*arguments)

    placed = (
        P("section", ("dp", "vit"), None),
        P("dp", None),
        P("dp", None),
        P(),
        P(("dp", "section", "vit"), None),
        P(("dp", "section", "vit"), None),
        P(),
        P(),
        P("section", None),
        P("section", None),
        P(),
        P(),
        P(None, "vit"),
        P("vit"),
        P("vit", None),
    )
    return jax.shard_map(
        chosen_form,
        mesh=mesh,
        in_specs=placed,
        out_specs=P(("dp", "section", "vit"), None),
        check_vma=False,
    )
```

```python
import jax
import jax.numpy as jnp
from jax import lax
from jax.experimental import pallas as pl
from jax.experimental.pallas import tpu as pltpu
from jax.sharding import PartitionSpec as P

HEADS = 16
LEVELS = 3


norm_eps = 1e-06


def normalize(values):
    row_mean = jnp.mean(values, axis=-1, keepdims=True)
    centered = values - row_mean
    variance = jnp.mean(centered * centered, axis=-1, keepdims=True)
    inverse = lax.rsqrt(variance + norm_eps)
    return (centered * inverse, inverse)


def normalize_back(upstream, normed_rows, inverse, gain):
    scaled = upstream * gain
    mean_scaled = jnp.mean(scaled, axis=-1, keepdims=True)
    mean_cross = jnp.mean(scaled * normed_rows, axis=-1, keepdims=True)
    return (scaled - mean_scaled - normed_rows * mean_cross) * inverse


def gelu_slope(pre_act):
    cumulative = 0.5 * (1.0 + lax.erf(pre_act * 0.7071067811865476))
    density = jnp.exp(-0.5 * pre_act * pre_act) * 0.3989422804014327
    return cumulative + pre_act * density


def local(
    grad_llm,
    vis_slot,
    image_rows,
    section_layer,
    vit_in,
    vit_out,
    ln_gain,
    ln_bias,
    qkv_weight,
    proj_weight,
    merge_gain,
    merge_bias,
    fc1_weight,
    fc1_bias,
    fc2_weight,
):
    sections = lax.axis_size("section")
    shards = lax.axis_size("vit")
    section_index = lax.axis_index("section")
    shard_index = lax.axis_index("vit")
    devices = sections * shards
    patches = vit_in.shape[0]
    slots_here = patches // 4
    run_rows = grad_llm.shape[1] // devices
    llm_width = grad_llm.shape[2]
    vit_width = vit_in.shape[1]
    head_dim = vit_width // HEADS
    device_index = section_index * shards + shard_index
    qkv_full, proj_full = (
        lax.all_gather(qkv_weight, "section", axis=0, tiled=True),
        lax.all_gather(proj_weight, "section", axis=0, tiled=True),
    )
    in_rows, in_inverse = normalize(vit_in.astype(jnp.float32))
    normed = (in_rows * ln_gain + ln_bias).astype(jnp.bfloat16)
    projected = lax.dot_general(
        qkv_full, normed, (((0,), (1,)), ((), ())), preferred_element_type=jnp.float32
    )
    projected = projected.astype(jnp.bfloat16).reshape(3, HEADS, head_dim, patches)
    section_weight = jnp.where(
        section_layer < LEVELS, (section_layer + 1).astype(jnp.float32) / LEVELS, 0.0
    )
    outgoing = grad_llm[0].reshape(devices, run_rows, llm_width)
    image_ends = jnp.cumsum(image_rows[section_index])
    out_rows, out_inverse = normalize(vit_out.astype(jnp.float32))
    merge_in = (
        (out_rows * merge_gain + merge_bias).astype(jnp.bfloat16).reshape(slots_here, 4 * vit_width)
    )
    arrived = lax.all_to_all(outgoing, ("section", "vit"), split_axis=0, concat_axis=0, tiled=True)
    arrived_f = arrived.reshape(sections, shards, run_rows, llm_width).astype(jnp.float32)
    incoming = jnp.sum(arrived_f * section_weight[:, None, None, None], axis=0)
    columns = lax.dynamic_slice_in_dim(vis_slot, device_index * run_rows, run_rows, 1)
    local_slot = (columns - device_index * slots_here).reshape(-1)
    placed = (
        jnp.zeros((slots_here, llm_width), jnp.float32)
        .at[local_slot]
        .set(incoming.reshape(-1, llm_width))
    )
    slot_position = shard_index * slots_here + jnp.arange(slots_here, dtype=jnp.int32)
    merged_grad = jnp.where((slot_position < image_ends[-1])[:, None], placed, 0.0).astype(
        jnp.bfloat16
    )
    rows_in, rows_grad = (
        lax.all_gather(merge_in, "vit", axis=0, tiled=True),
        lax.all_gather(merged_grad, "vit", axis=0, tiled=True),
    )
    pre_act = jnp.dot(rows_in, fc1_weight, preferred_element_type=jnp.float32) + fc1_bias
    hidden_grad = lax.dot_general(
        rows_grad, fc2_weight, (((1,), (1,)), ((), ())), preferred_element_type=jnp.float32
    )
    pre_grad = (hidden_grad * gelu_slope(pre_act)).astype(jnp.bfloat16)
    merge_grad = lax.psum_scatter(
        lax.dot_general(
            pre_grad, fc1_weight, (((1,), (1,)), ((), ())), preferred_element_type=jnp.float32
        ).astype(jnp.bfloat16),
        "vit",
        scatter_dimension=0,
        tiled=True,
    ).astype(jnp.float32)
    out_grad = normalize_back(
        merge_grad.reshape(patches, vit_width), out_rows, out_inverse, merge_gain
    ).astype(jnp.bfloat16)
    grad_cols = lax.dot_general(
        proj_full, out_grad, (((1,), (1,)), ((), ())), preferred_element_type=jnp.float32
    )
    grad_cols = grad_cols.astype(jnp.bfloat16).reshape(1, HEADS, head_dim, patches)
    head_inputs, head_grad = (
        lax.all_to_all(projected, "vit", split_axis=1, concat_axis=3, tiled=True),
        lax.all_to_all(grad_cols, "vit", split_axis=1, concat_axis=3, tiled=True),
    )
    length = shards * patches
    block_size = min(512, length)
    block_count = length // block_size
    slot_of = jnp.arange(length, dtype=jnp.int32) // 4
    patch_image = jnp.sum((slot_of[:, None] >= image_ends[None, :]).astype(jnp.int32), axis=1)
    patch_live = slot_of < image_ends[-1]
    score_scale = head_dim ** (-0.5)
    contract_first = (((0,), (0,)), ((), ()))

    def head_backward(query_cols, key_cols, value_cols, grad_head):

        def step(carry, block_index):
            key_acc, value_acc = carry
            first_row = block_index * block_size
            query_block = lax.dynamic_slice_in_dim(query_cols, first_row, block_size, 1)
            grad_block = lax.dynamic_slice_in_dim(grad_head, first_row, block_size, 1)
            image_block = lax.dynamic_slice_in_dim(patch_image, first_row, block_size, 0)
            live_block = lax.dynamic_slice_in_dim(patch_live, first_row, block_size, 0)
            scores = (
                lax.dot_general(
                    query_block, key_cols, contract_first, preferred_element_type=jnp.float32
                )
                * score_scale
            )
            allowed = (
                (image_block[:, None] == patch_image[None, :])
                & live_block[:, None]
                & patch_live[None, :]
            )
            exponent = jnp.where(allowed, jnp.exp(jnp.where(allowed, scores, 0.0)), 0.0)
            denominator = (
                jnp.sum(exponent, axis=1, keepdims=True)
                + 1.0
                - live_block.astype(jnp.float32)[:, None]
            )
            softmax_weights = (exponent / denominator).astype(jnp.bfloat16)
            prob_grad = lax.dot_general(
                grad_block, value_cols, contract_first, preferred_element_type=jnp.float32
            )
            weighted = softmax_weights.astype(jnp.float32)
            row_dot = jnp.sum(weighted * prob_grad, axis=1, keepdims=True)
            score_grad = (weighted * (prob_grad - row_dot) * score_scale).astype(jnp.bfloat16)
            query_grad = lax.dot_general(
                key_cols, score_grad, (((1,), (1,)), ((), ())), preferred_element_type=jnp.float32
            )
            key_acc = key_acc + lax.dot_general(
                query_block,
                score_grad,
                (((1,), (0,)), ((), ())),
                preferred_element_type=jnp.float32,
            )
            value_acc = value_acc + lax.dot_general(
                grad_block,
                softmax_weights,
                (((1,), (0,)), ((), ())),
                preferred_element_type=jnp.float32,
            )
            return ((key_acc, value_acc), query_grad.astype(jnp.bfloat16))

        empty = jnp.zeros((head_dim, length), jnp.float32)
        (key_total, value_total), query_blocks = lax.scan(
            step, (empty, empty), jnp.arange(block_count, dtype=jnp.int32)
        )
        query_total = query_blocks.transpose(1, 0, 2).reshape(head_dim, length)
        return (query_total, key_total.astype(jnp.bfloat16), value_total.astype(jnp.bfloat16))

    query_all, key_all, value_all = jax.vmap(head_backward)(
        head_inputs[0], head_inputs[1], head_inputs[2], head_grad[0]
    )
    head_result = jnp.stack([query_all, key_all, value_all])
    returned = lax.all_to_all(head_result, "vit", split_axis=3, concat_axis=1, tiled=True)
    projected_grad = returned.reshape(3 * vit_width, patches)
    normed_grad = lax.dot_general(
        projected_grad, qkv_full, (((0,), (1,)), ((), ())), preferred_element_type=jnp.float32
    )
    vit_grad = out_grad.astype(jnp.float32) + normalize_back(
        normed_grad, in_rows, in_inverse, ln_gain
    )
    return vit_grad.astype(jnp.bfloat16)


bf16, f32 = jnp.bfloat16, jnp.float32


def swap(values, axis, bit):
    count = lax.axis_size(axis)
    return lax.ppermute(values, axis, [(i, i ^ bit) for i in range(count)])


def fits(mesh, heads, head_dim, part_rows):
    sections, copies, shards = (mesh.shape[name] for name in ("section", "dp", "vit"))
    if (sections, copies, shards) != (4, 4, 2) or heads % (shards * copies):
        return False
    return part_rows % head_dim == 0 and heads // shards * head_dim % part_rows == 0


def dot(a, b, ca=1, cb=0):
    return lax.dot_general(a, b, (((ca,), (cb,)), ((), ())), preferred_element_type=f32)


def block_of(size, limit):
    return max(b for b in range(128, limit + 1, 128) if size % b == 0)


def run_kernel(body, grid, in_specs, out_specs, out_shape, scratch=(), prefetch=1):
    return pl.pallas_call(
        body,
        grid_spec=pltpu.PrefetchScalarGridSpec(
            num_scalar_prefetch=prefetch,
            grid=grid,
            in_specs=in_specs,
            out_specs=out_specs,
            scratch_shapes=list(scratch),
        ),
        out_shape=out_shape,
        compiler_params=pltpu.CompilerParams(
            dimension_semantics=("arbitrary",) * len(grid), vmem_limit_bytes=56 << 20
        ),
    )


def whole(array):
    return pl.BlockSpec(array.shape, lambda i, *_: (0,) * array.ndim)


def struct(shape, dtype):
    return jax.ShapeDtypeStruct(shape, dtype)


LANES = 128
AHEAD = 4


def put_rows(ref, first, values):
    for c in range(ref.shape[0]):
        ref[c, first : first + values.shape[0], :] = values[:, c * LANES : (c + 1) * LANES]


def every_fourth(ref, j, count):
    return jnp.concatenate(
        [ref[c, pl.ds(j, count, stride=4), :] for c in range(ref.shape[0])], axis=1
    )


def weighted_sum(place, weights, grad_llm, arrived):
    rows, width = arrived[0].shape

    def body(place_ref, weight_ref, own_ref, *refs):
        here = place_ref[0]
        total = weight_ref[here] * own_ref[0].astype(f32)
        for k, ref in enumerate(refs[:-1]):
            total += weight_ref[here ^ (k + 1)] * ref[...].astype(f32)
        refs[-1][...] = total.astype(bf16)

    return run_kernel(
        body,
        (1,),
        [pl.BlockSpec((1, rows, width), lambda i, place, w: (0, place[0], 0))]
        + [whole(x) for x in arrived],
        pl.BlockSpec((rows, width), lambda i, *_: (0, 0)),
        struct((rows, width), bf16),
        prefetch=2,
    )(place, weights, grad_llm, *arrived)


def streamed(source, buffer, sems, index, block, axis):
    window = pl.ds(pl.multiple_of(index * block, LANES), block)
    part = source.at[window, :] if axis == 0 else source.at[:, window]
    return pltpu.make_async_copy(part, buffer.at[index], sems.at[index])


def slope_of(place, own, other, params, fc1_weight):
    patches, width = own.shape
    slots = patches * 2 // 4
    depth, hidden = fc1_weight.shape
    block = block_of(hidden, 256)
    steps = hidden // block
    ahead = min(AHEAD, steps)

    def body(place_ref, own_ref, other_ref, param_ref, fc1_ref, out_ref, x, m, buffer, sems):
        def fetch(i):
            return streamed(fc1_ref, buffer, sems, i, block, 1)

        for i in range(ahead):
            fetch(i).start()
        put_rows(x, 0, own_ref[...].astype(f32))
        put_rows(x, patches, other_ref[...].astype(f32))
        gain, bias = param_ref[0:1, :width], param_ref[1:2, :width]
        for j in range(4):
            rows, _ = normalize(every_fourth(x, j, slots))
            m[:, j * width : (j + 1) * width] = (rows * gain + bias).astype(bf16)

        def step(i, carry):
            fetch(i).wait()

            @pl.when(i + ahead < steps)
            def _():
                fetch(i + ahead).start()

            window = pl.ds(pl.multiple_of(i * block, LANES), block)
            pre_act = dot(m[...], buffer[i]) + param_ref[4:5, window]
            out_ref[:, window] = gelu_slope(pre_act)
            return carry

        lax.fori_loop(0, steps, step, 0)

    return run_kernel(
        body,
        (1,),
        [whole(own), whole(other), whole(params), pl.BlockSpec(memory_space=pl.ANY)],
        pl.BlockSpec((slots, hidden), lambda i, _: (0, 0)),
        struct((slots, hidden), f32),
        [
            pltpu.VMEM((width // LANES, 2 * patches, LANES), f32),
            pltpu.VMEM((slots, depth), bf16),
            pltpu.VMEM((steps, depth, block), bf16),
            pltpu.SemaphoreType.DMA((steps,)),
        ],
    )(place, own, other, params, fc1_weight)


def merge_first(place, chosen, own, other, fc2_weight, slope, fc1_weight, parts):
    rows, width = own.shape
    slots, hidden = slope.shape
    columns = fc1_weight.shape[0] // parts
    block2, block1 = block_of(hidden, 256), block_of(columns, 384)
    steps2, steps1 = hidden // block2, columns // block1
    ahead = min(AHEAD, steps2, steps1)

    def body(
        place_ref, chosen_ref, own_ref, other_ref, slope_ref, fc2_ref, fc1_ref,
        pre_ref, out_ref, merged, buffer2, buffer1, sems2, sems1,
    ):
        def fetch2(i):
            return streamed(fc2_ref, buffer2, sems2, i, block2, 0)

        def fetch1(i):
            return streamed(fc1_ref, buffer1, sems1, i, block1, 0)

        for i in range(ahead):
            fetch2(i).start()
        both = jnp.concatenate([own_ref[...], other_ref[...]], axis=0)
        merged[...] = dot(chosen_ref[...], both).astype(bf16)

        def step2(i, carry):
            fetch2(i).wait()

            @pl.when(i + ahead < steps2)
            def _():
                fetch2(i + ahead).start()

            @pl.when(i + ahead >= steps2)
            def _():
                fetch1(i + ahead - steps2).start()

            window = pl.ds(pl.multiple_of(i * block2, LANES), block2)
            hidden_grad = dot(merged[...], buffer2[i], 1, 1)
            pre_ref[:, window] = (hidden_grad * slope_ref[:, window]).astype(bf16)
            return carry

        def step1(i, carry):
            fetch1(i).wait()

            @pl.when(i + ahead < steps1)
            def _():
                fetch1(i + ahead).start()

            window = pl.ds(pl.multiple_of(i * block1, LANES), block1)
            out_ref[:, window] = dot(pre_ref[...], buffer1[i], 1, 1).astype(bf16)
            return carry

        lax.fori_loop(0, steps2, step2, 0)
        lax.fori_loop(0, steps1, step1, 0)

    return run_kernel(
        body,
        (1,),
        [whole(x) for x in (chosen, own, other, slope)]
        + [pl.BlockSpec(memory_space=pl.ANY)] * 2,
        [
            pl.BlockSpec((slots, hidden), lambda i, _: (0, 0)),
            pl.BlockSpec((slots, columns), lambda i, _: (0, 0)),
        ],
        [struct((slots, hidden), bf16), struct((slots, columns), bf16)],
        [
            pltpu.VMEM((slots, width), bf16),
            pltpu.VMEM((steps2, block2, width), bf16),
            pltpu.VMEM((steps1, block1, hidden), bf16),
            pltpu.SemaphoreType.DMA((steps2,)),
            pltpu.SemaphoreType.DMA((steps1,)),
        ],
    )(place, chosen, own, other, slope, fc2_weight, fc1_weight)


def merge_next(place, pre_grad, fc1_weight, part, parts):
    slots, hidden = pre_grad.shape
    columns = fc1_weight.shape[0] // parts
    block = block_of(columns, 384)
    steps = columns // block
    ahead = min(AHEAD, steps)

    def body(place_ref, pre_ref, fc1_ref, out_ref, buffer, sems):
        def fetch(i):
            window = pl.ds(pl.multiple_of(part * columns + i * block, LANES), block)
            return pltpu.make_async_copy(fc1_ref.at[window, :], buffer.at[i], sems.at[i])

        for i in range(ahead):
            fetch(i).start()

        def step(i, carry):
            fetch(i).wait()

            @pl.when(i + ahead < steps)
            def _():
                fetch(i + ahead).start()

            window = pl.ds(pl.multiple_of(i * block, LANES), block)
            out_ref[:, window] = dot(pre_ref[...], buffer[i], 1, 1).astype(bf16)
            return carry

        lax.fori_loop(0, steps, step, 0)

    return run_kernel(
        body,
        (1,),
        [whole(pre_grad), pl.BlockSpec(memory_space=pl.ANY)],
        pl.BlockSpec((slots, columns), lambda i, _: (0, 0)),
        struct((slots, columns), bf16),
        [pltpu.VMEM((steps, block, hidden), bf16), pltpu.SemaphoreType.DMA((steps,))],
    )(place, pre_grad, fc1_weight)


def project(place, own, other, params, weights, head_dim):
    patches, width = own.shape
    length = 2 * patches
    slots = length // 4
    sections, copies = len(weights), len(weights[0])
    part_rows, group_cols = weights[0][0].shape
    pieces = group_cols // head_dim
    flat = [w for parts in weights for w in parts]

    def body(place_ref, own_ref, other_ref, param_ref, *refs):
        w_refs, (out_ref, x, n) = refs[: len(flat)], refs[len(flat) :]
        put_rows(x, 0, own_ref[...].astype(f32))
        put_rows(x, patches, other_ref[...].astype(f32))
        gain, bias = param_ref[2:3, :width], param_ref[3:4, :width]
        for j in range(4):
            rows, _ = normalize(every_fourth(x, j, slots))
            rows = (rows * gain + bias).astype(bf16)
            for t in range(sections):
                n[t, j * slots : (j + 1) * slots, :] = rows[:, t * part_rows : (t + 1) * part_rows]
        for p in range(copies):
            total = sum(
                dot(n[place_ref[0] ^ k], w_refs[k * copies + p][:, :group_cols])
                for k in range(sections)
            ).T
            for c in range(pieces):
                out_ref[p, c] = total[c * head_dim : (c + 1) * head_dim].astype(bf16)

    shape = (copies, pieces, head_dim, length)
    return run_kernel(
        body,
        (1,),
        [whole(x) for x in (own, other, params, *flat)],
        pl.BlockSpec(shape, lambda i, _: (0, 0, 0, 0)),
        struct(shape, bf16),
        [
            pltpu.VMEM((width // LANES, length, LANES), f32),
            pltpu.VMEM((sections, length, part_rows), bf16),
        ],
    )(place, own, other, params, *flat)


def attention_back(
    place, own, other, params, mine, theirs, proj_weight, projected, weights, head_dim, images
):
    patches, width = own.shape
    length = 2 * patches
    slots = length // 4
    half = slots // 2
    sections, copies = len(weights), len(weights[0])
    part_rows, group_cols = weights[0][0].shape
    group_heads = group_cols // (3 * head_dim)
    part_heads = part_rows // head_dim
    shard_sections = copies * group_heads // part_heads
    flat = [w for parts in weights for w in parts]
    chunks = len(mine)
    per_chunk = 4 // chunks
    score_scale = head_dim ** (-0.5)

    def body(place_ref, own_ref, other_ref, param_ref, *refs):
        gain = param_ref[0:1, :width]
        mine_refs, refs = refs[:chunks], refs[chunks:]
        theirs_refs, refs = refs[:chunks], refs[chunks:]
        proj_ref, projected_ref, refs = refs[0], refs[1], refs[2:]
        w_refs, refs = refs[: len(flat)], refs[len(flat) :]
        own_out, other_out, grad_out, x, og, og_parts, heads, acc = refs
        section, shard, copy = place_ref[0], place_ref[1], place_ref[2]
        put_rows(x, 0, own_ref[...].astype(f32))
        put_rows(x, patches, other_ref[...].astype(f32))
        for j in range(4):
            rows, inverse = normalize(every_fourth(x, j, slots))
            cols = slice(j % per_chunk * width, (j % per_chunk + 1) * width)
            there = theirs_refs[j // per_chunk][:, cols]
            there = jnp.concatenate([there[half:], there[:half]], axis=0)
            upstream = mine_refs[j // per_chunk][:, cols].astype(f32) + there.astype(f32)
            result = normalize_back(upstream, rows, inverse, gain).astype(bf16)
            og[j * slots : (j + 1) * slots, :] = result
            grad_out[j] = result[:half]
            for t in range(sections):
                og_parts[t, j * slots : (j + 1) * slots, :] = result[
                    :, t * part_rows : (t + 1) * part_rows
                ]

        for i in range(shard_sections):
            relation = section ^ (shard * shard_sections + i)
            for k in range(sections):

                @pl.when(relation == k)
                def _(i=i, k=k):
                    if k == 0:
                        cols = dot(proj_ref[...], og[...], 1, 1)
                    else:
                        cols = sum(
                            dot(
                                w_refs[k * copies + p][:, group_cols : group_cols + part_rows],
                                og_parts[copy ^ p],
                                1,
                                1,
                            )
                            for p in range(copies)
                        )
                    for h in range(part_heads):
                        heads[i * part_heads + h] = cols[h * head_dim : (h + 1) * head_dim].astype(bf16)

        def image_of(axis):
            index = lax.broadcasted_iota(jnp.int32, (length, length), axis) % slots
            position = ((index // half) ^ shard) * half + index % half
            image = jnp.zeros((length, length), jnp.int32)
            for e in range(images):
                image += (position >= place_ref[3 + e]).astype(jnp.int32)
            return image

        image = image_of(0)
        allowed = (image == image_of(1)) & (image < images)
        dead = (image_of(1)[:1] == images).astype(f32)
        for p in range(copies):
            grads = [[], [], []]
            for h in range(group_heads):
                query, key, value = (projected_ref[p, c * group_heads + h] for c in range(3))
                grad = heads[(copy ^ p) * group_heads + h]
                scores = dot(key, query, 0, 0) * score_scale
                exponent = jnp.where(allowed, jnp.exp(scores), 0.0)
                denominator = jnp.sum(exponent, axis=0, keepdims=True) + dead
                softmax_weights = (exponent / denominator).astype(bf16)
                prob_grad = dot(value, grad, 0, 0)
                weighted = softmax_weights.astype(f32)
                row_dot = jnp.sum(weighted * prob_grad, axis=0, keepdims=True)
                score_grad = (weighted * (prob_grad - row_dot) * score_scale).astype(bf16)
                grads[0].append(dot(key, score_grad))
                grads[1].append(dot(query, score_grad, 1, 1))
                grads[2].append(dot(grad, softmax_weights, 1, 1))
            group_grad = jnp.concatenate([g for gs in grads for g in gs], axis=0).astype(bf16)
            for k in range(sections):
                term = dot(w_refs[k * copies + p][:, :group_cols], group_grad)
                acc[k] = term if p == 0 else acc[k] + term

        result = jnp.concatenate([acc[section ^ t] for t in range(sections)], axis=0).T
        for j in range(4):
            own_out[j] = result[j * slots : j * slots + half]
            other_out[j] = result[j * slots + half : (j + 1) * slots].astype(bf16)

    shape = (4, half, width)
    operands = (own, other, params, *mine, *theirs, proj_weight, projected, *flat)
    return run_kernel(
        body,
        (1,),
        [whole(x) for x in operands],
        [pl.BlockSpec(shape, lambda i, _: (0, 0, 0))] * 3,
        [struct(shape, f32), struct(shape, bf16), struct(shape, bf16)],
        [
            pltpu.VMEM((width // LANES, length, LANES), f32),
            pltpu.VMEM((length, width), bf16),
            pltpu.VMEM((sections, length, part_rows), bf16),
            pltpu.VMEM((copies * group_heads, head_dim, length), bf16),
            pltpu.VMEM((sections, part_rows, length), f32),
        ],
    )(place, *operands)


def finish(place, own, params, mine, theirs, out_grad):
    patches, width = own.shape

    def body(place_ref, own_ref, param_ref, mine_ref, theirs_ref, grad_ref, out_ref, x):
        gain = param_ref[2:3, :width]
        put_rows(x, 0, own_ref[...].astype(f32))
        for j in range(4):
            rows, inverse = normalize(every_fourth(x, j, patches // 4))
            upstream = mine_ref[j] + theirs_ref[j].astype(f32)
            result = grad_ref[j].astype(f32) + normalize_back(
                upstream, rows, inverse, gain
            )
            for c in range(x.shape[0]):
                x[c, pl.ds(j, patches // 4, stride=4), :] = result[:, c * LANES : (c + 1) * LANES]
        out_ref[...] = jnp.concatenate([x[c] for c in range(x.shape[0])], axis=1).astype(bf16)

    operands = (own, params, mine, theirs, out_grad)
    return run_kernel(
        body,
        (1,),
        [whole(x) for x in operands],
        pl.BlockSpec((patches, width), lambda i, _: (0, 0)),
        struct((patches, width), bf16),
        [pltpu.VMEM((width // LANES, patches, LANES), f32)],
    )(place, *operands)


def local_paired(
    grad_llm,
    vis_slot,
    image_rows,
    section_layer,
    vit_in,
    vit_out,
    ln_gain,
    ln_bias,
    qkv_weight,
    proj_weight,
    merge_gain,
    merge_bias,
    fc1_weight,
    fc1_bias,
    fc2_weight,
):
    sections = lax.axis_size("section")
    shards = lax.axis_size("vit")
    copies = lax.axis_size("dp")
    section_index = lax.axis_index("section")
    shard_index = lax.axis_index("vit")
    copy_index = lax.axis_index("dp")
    patches = vit_in.shape[0]
    slots_here = patches // 4
    llm_width = grad_llm.shape[2]
    vit_width = vit_in.shape[1]
    head_dim = vit_width // HEADS
    part_rows = qkv_weight.shape[0]
    group_heads = HEADS // (shards * copies)
    group_rows = grad_llm.shape[1] // sections
    images = image_rows.shape[1]
    image_ends = jnp.cumsum(image_rows[section_index]).astype(jnp.int32)
    place = jnp.concatenate(
        [jnp.stack([section_index, shard_index, copy_index]).astype(jnp.int32), image_ends]
    )
    hidden = fc1_bias.shape[0]
    params = jnp.stack(
        [jnp.pad(x, (0, hidden - vit_width)) for x in (merge_gain, merge_bias, ln_gain, ln_bias)]
        + [fc1_bias]
    )

    outgoing = grad_llm[0].reshape(sections, group_rows, llm_width)
    vit_out_other = swap(vit_out, "vit", 1)
    arrived = [
        swap(lax.dynamic_index_in_dim(outgoing, section_index ^ k, 0, keepdims=False), "section", k)
        for k in range(1, sections)
    ]

    def own_group(p, source=qkv_weight):
        first = (shard_index * copies + (copy_index ^ p)) * group_heads * head_dim
        return [
            lax.dynamic_slice_in_dim(source, c * vit_width + first, group_heads * head_dim, 1)
            for c in range(3)
        ]

    proj_cols = lax.dynamic_slice_in_dim(proj_weight, copy_index * part_rows, part_rows, 1)
    piece = jnp.concatenate([*own_group(0), proj_cols], axis=1)
    near = swap(piece, "section", 1)

    slope = slope_of(place, vit_out, vit_out_other, params, fc1_weight)
    arrived, slope, piece, qkv_later = lax.optimization_barrier(
        (arrived, slope, piece, qkv_weight)
    )
    far = swap(piece, "section", 2)

    section_weight = jnp.where(
        section_layer < LEVELS, (section_layer + 1).astype(f32) / LEVELS, 0.0
    )
    summed = weighted_sum(place, section_weight, grad_llm, arrived)
    summed_other = swap(summed, "vit", 1)
    near_chip = swap(near, "dp", 2)
    own_parts = [jnp.concatenate(own_group(p, qkv_later), axis=1) for p in range(copies)]
    halves = jnp.arange(shards, dtype=jnp.int32) ^ shard_index
    slot_position = (
        halves[:, None] * slots_here + jnp.arange(slots_here, dtype=jnp.int32)
    ).reshape(-1)
    named = lax.dynamic_slice_in_dim(vis_slot, section_index * group_rows, group_rows, 1)
    named = jnp.where(shard_index == 0, named, named[::-1]).reshape(-1)
    named = named - section_index * shards * slots_here
    chosen = (slot_position[:, None] == named[None, :]) & (slot_position < image_ends[-1])[:, None]

    pre_grad, first = merge_first(
        place, chosen.astype(bf16), summed, summed_other, fc2_weight, slope, fc1_weight, 2
    )
    first, far, near, near_chip, vit_in_sent = lax.optimization_barrier(
        (first, far, near, near_chip, vit_in)
    )
    first_theirs = swap(first, "vit", 1)
    cross = swap(far, "section", 1)
    far_chip = swap(far, "dp", 2)
    near_core, near_diagonal = swap(near, "dp", 1), swap(near_chip, "dp", 1)
    vit_in_other = swap(vit_in_sent, "vit", 1)
    second = merge_next(place, pre_grad, fc1_weight, 1, 2)
    second, cross, far_chip = lax.optimization_barrier((second, cross, far_chip))
    second_theirs = swap(second, "vit", 1)
    cross_chip = swap(cross, "dp", 2)
    far_core, far_diagonal = swap(far, "dp", 1), swap(far_chip, "dp", 1)
    cross_core, cross_diagonal = swap(cross, "dp", 1), swap(cross_chip, "dp", 1)
    weights = [
        own_parts,
        [near, near_core, near_chip, near_diagonal],
        [far, far_core, far_chip, far_diagonal],
        [cross, cross_core, cross_chip, cross_diagonal],
    ]

    projected = project(place, vit_in, vit_in_other, params, weights, head_dim)
    normed_mine, normed_sent, out_grad = attention_back(
        place,
        vit_out,
        vit_out_other,
        params,
        [first, second],
        [first_theirs, second_theirs],
        proj_weight,
        projected,
        weights,
        head_dim,
        images,
    )
    normed_theirs = swap(normed_sent, "vit", 1)
    return finish(place, vit_in, params, normed_mine, normed_theirs, out_grad)


def solution(mesh):
    def chosen_form(*arguments):
        width, part_rows = arguments[4].shape[1], arguments[8].shape[0]
        paired = fits(mesh, HEADS, width // HEADS, part_rows)
        return (local_paired if paired else local)(*arguments)

    placed = (
        P("section", ("dp", "vit"), None),
        P("dp", None),
        P("dp", None),
        P(),
        P(("dp", "section", "vit"), None),
        P(("dp", "section", "vit"), None),
        P(),
        P(),
        P("section", None),
        P("section", None),
        P(),
        P(),
        P(None, "vit"),
        P("vit"),
        P("vit", None),
    )
    return jax.shard_map(
        chosen_form,
        mesh=mesh,
        in_specs=placed,
        out_specs=P(("dp", "section", "vit"), None),
        check_vma=False,
    )
```

```python
import jax
import jax.numpy as jnp
from jax import lax
from jax.experimental import pallas as pl
from jax.experimental.pallas import tpu as pltpu
from jax.sharding import PartitionSpec as P

HEADS = 16
LEVELS = 3


norm_eps = 1e-06


def normalize(values):
    row_mean = jnp.mean(values, axis=-1, keepdims=True)
    centered = values - row_mean
    variance = jnp.mean(centered * centered, axis=-1, keepdims=True)
    inverse = lax.rsqrt(variance + norm_eps)
    return (centered * inverse, inverse)


def normalize_back(upstream, normed_rows, inverse, gain):
    scaled = upstream * gain
    mean_scaled = jnp.mean(scaled, axis=-1, keepdims=True)
    mean_cross = jnp.mean(scaled * normed_rows, axis=-1, keepdims=True)
    return (scaled - mean_scaled - normed_rows * mean_cross) * inverse


def gelu_slope(pre_act):
    cumulative = 0.5 * (1.0 + lax.erf(pre_act * 0.7071067811865476))
    density = jnp.exp(-0.5 * pre_act * pre_act) * 0.3989422804014327
    return cumulative + pre_act * density


def local(
    grad_llm,
    vis_slot,
    image_rows,
    section_layer,
    vit_in,
    vit_out,
    ln_gain,
    ln_bias,
    qkv_weight,
    proj_weight,
    merge_gain,
    merge_bias,
    fc1_weight,
    fc1_bias,
    fc2_weight,
):
    sections = lax.axis_size("section")
    shards = lax.axis_size("vit")
    section_index = lax.axis_index("section")
    shard_index = lax.axis_index("vit")
    devices = sections * shards
    patches = vit_in.shape[0]
    slots_here = patches // 4
    run_rows = grad_llm.shape[1] // devices
    llm_width = grad_llm.shape[2]
    vit_width = vit_in.shape[1]
    head_dim = vit_width // HEADS
    device_index = section_index * shards + shard_index
    qkv_full, proj_full = (
        lax.all_gather(qkv_weight, "section", axis=0, tiled=True),
        lax.all_gather(proj_weight, "section", axis=0, tiled=True),
    )
    in_rows, in_inverse = normalize(vit_in.astype(jnp.float32))
    normed = (in_rows * ln_gain + ln_bias).astype(jnp.bfloat16)
    projected = lax.dot_general(
        qkv_full, normed, (((0,), (1,)), ((), ())), preferred_element_type=jnp.float32
    )
    projected = projected.astype(jnp.bfloat16).reshape(3, HEADS, head_dim, patches)
    section_weight = jnp.where(
        section_layer < LEVELS, (section_layer + 1).astype(jnp.float32) / LEVELS, 0.0
    )
    outgoing = grad_llm[0].reshape(devices, run_rows, llm_width)
    image_ends = jnp.cumsum(image_rows[section_index])
    out_rows, out_inverse = normalize(vit_out.astype(jnp.float32))
    merge_in = (
        (out_rows * merge_gain + merge_bias).astype(jnp.bfloat16).reshape(slots_here, 4 * vit_width)
    )
    arrived = lax.all_to_all(outgoing, ("section", "vit"), split_axis=0, concat_axis=0, tiled=True)
    arrived_f = arrived.reshape(sections, shards, run_rows, llm_width).astype(jnp.float32)
    incoming = jnp.sum(arrived_f * section_weight[:, None, None, None], axis=0)
    columns = lax.dynamic_slice_in_dim(vis_slot, device_index * run_rows, run_rows, 1)
    local_slot = (columns - device_index * slots_here).reshape(-1)
    placed = (
        jnp.zeros((slots_here, llm_width), jnp.float32)
        .at[local_slot]
        .set(incoming.reshape(-1, llm_width))
    )
    slot_position = shard_index * slots_here + jnp.arange(slots_here, dtype=jnp.int32)
    merged_grad = jnp.where((slot_position < image_ends[-1])[:, None], placed, 0.0).astype(
        jnp.bfloat16
    )
    rows_in, rows_grad = (
        lax.all_gather(merge_in, "vit", axis=0, tiled=True),
        lax.all_gather(merged_grad, "vit", axis=0, tiled=True),
    )
    pre_act = jnp.dot(rows_in, fc1_weight, preferred_element_type=jnp.float32) + fc1_bias
    hidden_grad = lax.dot_general(
        rows_grad, fc2_weight, (((1,), (1,)), ((), ())), preferred_element_type=jnp.float32
    )
    pre_grad = (hidden_grad * gelu_slope(pre_act)).astype(jnp.bfloat16)
    merge_grad = lax.psum_scatter(
        lax.dot_general(
            pre_grad, fc1_weight, (((1,), (1,)), ((), ())), preferred_element_type=jnp.float32
        ).astype(jnp.bfloat16),
        "vit",
        scatter_dimension=0,
        tiled=True,
    ).astype(jnp.float32)
    out_grad = normalize_back(
        merge_grad.reshape(patches, vit_width), out_rows, out_inverse, merge_gain
    ).astype(jnp.bfloat16)
    grad_cols = lax.dot_general(
        proj_full, out_grad, (((1,), (1,)), ((), ())), preferred_element_type=jnp.float32
    )
    grad_cols = grad_cols.astype(jnp.bfloat16).reshape(1, HEADS, head_dim, patches)
    head_inputs, head_grad = (
        lax.all_to_all(projected, "vit", split_axis=1, concat_axis=3, tiled=True),
        lax.all_to_all(grad_cols, "vit", split_axis=1, concat_axis=3, tiled=True),
    )
    length = shards * patches
    block_size = min(512, length)
    block_count = length // block_size
    slot_of = jnp.arange(length, dtype=jnp.int32) // 4
    patch_image = jnp.sum((slot_of[:, None] >= image_ends[None, :]).astype(jnp.int32), axis=1)
    patch_live = slot_of < image_ends[-1]
    score_scale = head_dim ** (-0.5)
    contract_first = (((0,), (0,)), ((), ()))

    def head_backward(query_cols, key_cols, value_cols, grad_head):

        def step(carry, block_index):
            key_acc, value_acc = carry
            first_row = block_index * block_size
            query_block = lax.dynamic_slice_in_dim(query_cols, first_row, block_size, 1)
            grad_block = lax.dynamic_slice_in_dim(grad_head, first_row, block_size, 1)
            image_block = lax.dynamic_slice_in_dim(patch_image, first_row, block_size, 0)
            live_block = lax.dynamic_slice_in_dim(patch_live, first_row, block_size, 0)
            scores = (
                lax.dot_general(
                    query_block, key_cols, contract_first, preferred_element_type=jnp.float32
                )
                * score_scale
            )
            allowed = (
                (image_block[:, None] == patch_image[None, :])
                & live_block[:, None]
                & patch_live[None, :]
            )
            exponent = jnp.where(allowed, jnp.exp(jnp.where(allowed, scores, 0.0)), 0.0)
            denominator = (
                jnp.sum(exponent, axis=1, keepdims=True)
                + 1.0
                - live_block.astype(jnp.float32)[:, None]
            )
            softmax_weights = (exponent / denominator).astype(jnp.bfloat16)
            prob_grad = lax.dot_general(
                grad_block, value_cols, contract_first, preferred_element_type=jnp.float32
            )
            weighted = softmax_weights.astype(jnp.float32)
            row_dot = jnp.sum(weighted * prob_grad, axis=1, keepdims=True)
            score_grad = (weighted * (prob_grad - row_dot) * score_scale).astype(jnp.bfloat16)
            query_grad = lax.dot_general(
                key_cols, score_grad, (((1,), (1,)), ((), ())), preferred_element_type=jnp.float32
            )
            key_acc = key_acc + lax.dot_general(
                query_block,
                score_grad,
                (((1,), (0,)), ((), ())),
                preferred_element_type=jnp.float32,
            )
            value_acc = value_acc + lax.dot_general(
                grad_block,
                softmax_weights,
                (((1,), (0,)), ((), ())),
                preferred_element_type=jnp.float32,
            )
            return ((key_acc, value_acc), query_grad.astype(jnp.bfloat16))

        empty = jnp.zeros((head_dim, length), jnp.float32)
        (key_total, value_total), query_blocks = lax.scan(
            step, (empty, empty), jnp.arange(block_count, dtype=jnp.int32)
        )
        query_total = query_blocks.transpose(1, 0, 2).reshape(head_dim, length)
        return (query_total, key_total.astype(jnp.bfloat16), value_total.astype(jnp.bfloat16))

    query_all, key_all, value_all = jax.vmap(head_backward)(
        head_inputs[0], head_inputs[1], head_inputs[2], head_grad[0]
    )
    head_result = jnp.stack([query_all, key_all, value_all])
    returned = lax.all_to_all(head_result, "vit", split_axis=3, concat_axis=1, tiled=True)
    projected_grad = returned.reshape(3 * vit_width, patches)
    normed_grad = lax.dot_general(
        projected_grad, qkv_full, (((0,), (1,)), ((), ())), preferred_element_type=jnp.float32
    )
    vit_grad = out_grad.astype(jnp.float32) + normalize_back(
        normed_grad, in_rows, in_inverse, ln_gain
    )
    return vit_grad.astype(jnp.bfloat16)


bf16, f32 = jnp.bfloat16, jnp.float32


def swap(values, axis, bit):
    count = lax.axis_size(axis)
    return lax.ppermute(values, axis, [(i, i ^ bit) for i in range(count)])


def fits(mesh):
    sections, copies, shards = (mesh.shape[name] for name in ("section", "dp", "vit"))
    return (sections, copies, shards) == (4, 4, 2)


def dot(a, b, ca=1, cb=0):
    return lax.dot_general(a, b, (((ca,), (cb,)), ((), ())), preferred_element_type=f32)


def block_of(size, limit):
    return max(b for b in range(128, limit + 1, 128) if size % b == 0)


def run_kernel(body, grid, in_specs, out_specs, out_shape, scratch=(), prefetch=0, limit=10):
    return pl.pallas_call(
        body,
        grid_spec=pltpu.PrefetchScalarGridSpec(
            num_scalar_prefetch=prefetch,
            grid=grid,
            in_specs=in_specs,
            out_specs=out_specs,
            scratch_shapes=list(scratch),
        ),
        out_shape=out_shape,
        compiler_params=pltpu.CompilerParams(
            dimension_semantics=("arbitrary",) * len(grid), vmem_limit_bytes=limit << 20
        ),
    )


def whole(array):
    return pl.BlockSpec(array.shape, lambda i, *_: (0,) * array.ndim)


RESIDENT = pl.BlockSpec(memory_space=pltpu.VMEM)


def struct(shape, dtype):
    return jax.ShapeDtypeStruct(shape, dtype)


LANES = 128


def put_rows(ref, first, values):
    for c in range(ref.shape[0]):
        ref[c, first : first + values.shape[0], :] = values[:, c * LANES : (c + 1) * LANES]


def every_fourth(ref, j, count):
    return jnp.concatenate(
        [ref[c, pl.ds(j, count, stride=4), :] for c in range(ref.shape[0])], axis=1
    )


def image_ends(image_ref, images):
    group, ends = lax.axis_index("section"), []
    for k in range(images):
        ends.append(image_ref[k, group] + (ends[-1] if ends else 0))
    return ends


def weighted_sum(section_layer, grad_llm, arrived):
    rows, width = arrived[0].shape

    def body(layer_ref, grad_ref, *refs):
        arrived_refs, (out_ref, own, sem) = refs[:-3], refs[-3:]
        here = lax.axis_index("section")
        window = pl.ds(pl.multiple_of(here * rows, 16), rows)
        copy = pltpu.make_async_copy(grad_ref.at[0, window, :], own, sem)
        copy.start()

        def term(section, values):
            layer = layer_ref[section]
            weight = jnp.where(layer < LEVELS, (layer + 1).astype(f32) / LEVELS, 0.0)
            return weight * values.astype(f32)

        total = sum(term(here ^ (k + 1), ref[...]) for k, ref in enumerate(arrived_refs))
        copy.wait()
        out_ref[...] = (total + term(here, own[...])).astype(bf16)

    return run_kernel(
        body,
        (1,),
        [pl.BlockSpec(memory_space=pl.ANY)] + [whole(x) for x in arrived],
        pl.BlockSpec((rows, width), lambda i, *_: (0, 0)),
        struct((rows, width), bf16),
        [pltpu.VMEM((rows, width), bf16), pltpu.SemaphoreType.DMA],
        prefetch=1,
    )(section_layer, grad_llm, *arrived)


def slope_of(own, other, gain, bias, fc1_weight, fc1_bias):
    patches, width = own.shape
    slots = patches * 2 // 4
    depth, hidden = fc1_weight.shape
    block = block_of(hidden, 256)
    steps = hidden // block

    def body(own_ref, other_ref, gain_ref, bias_ref, fc1b_ref, fc1_ref, out_ref, x, m):
        put_rows(x, 0, own_ref[...].astype(f32))
        put_rows(x, patches, other_ref[...].astype(f32))
        gain, bias = gain_ref[...].reshape(1, width), bias_ref[...].reshape(1, width)
        for j in range(4):
            rows, _ = normalize(every_fourth(x, j, slots))
            m[:, j * width : (j + 1) * width] = (rows * gain + bias).astype(bf16)

        def step(i, carry):
            window = pl.ds(pl.multiple_of(i * block, LANES), block)
            pre_act = dot(m[...], fc1_ref[:, window]) + fc1b_ref[window].reshape(1, block)
            out_ref[:, window] = gelu_slope(pre_act)
            return carry

        lax.fori_loop(0, steps, step, 0)

    return run_kernel(
        body,
        (1,),
        [whole(x) for x in (own, other, gain, bias, fc1_bias)]
        + [RESIDENT],
        pl.BlockSpec((slots, hidden), lambda i, *_: (0, 0)),
        struct((slots, hidden), f32),
        [
            pltpu.VMEM((width // LANES, 2 * patches, LANES), f32),
            pltpu.VMEM((slots, depth), bf16),
        ],
    )(own, other, gain, bias, fc1_bias, fc1_weight)


def pre_grad_of(image_rows, vis_slot, own, other, fc2_weight, slope):
    rows, width = own.shape
    slots, hidden = slope.shape
    half = slots // 2
    llm_rows = vis_slot.shape[1]
    images = image_rows.shape[0]
    block = block_of(hidden, 256)
    steps = hidden // block

    def body(image_ref, slot_ref, own_ref, other_ref, slope_ref, fc2_ref, out_ref, merged):
        section, shard = lax.axis_index("section"), lax.axis_index("vit")
        index = lax.broadcasted_iota(jnp.int32, (slots, llm_rows), 0)
        position = ((index // half) ^ shard) * half + index % half
        live = position < image_ends(image_ref, images)[-1]
        shift = (
            lax.broadcasted_iota(jnp.int32, (llm_rows, rows), 0)
            == lax.broadcasted_iota(jnp.int32, (llm_rows, rows), 1) + section * rows
        ).astype(bf16)
        chosen = []
        for part in range(2):
            named = slot_ref[pl.ds(shard ^ part, 1), :] - section * slots
            found = ((position == named) & live).astype(f32).astype(bf16)
            chosen.append(dot(found, shift))
        chosen = jnp.concatenate(chosen, axis=1).astype(bf16)
        total = dot(chosen, jnp.concatenate([own_ref[...], other_ref[...]], axis=0))
        merged[...] = total.astype(bf16)

        def step(i, carry):
            window = pl.ds(pl.multiple_of(i * block, LANES), block)
            hidden_grad = dot(merged[...], fc2_ref[window, :], 1, 1)
            out_ref[:, window] = (hidden_grad * slope_ref[:, window]).astype(bf16)
            return carry

        lax.fori_loop(0, steps, step, 0)

    return run_kernel(
        body,
        (1,),
        [whole(x) for x in (vis_slot, own, other, slope)] + [RESIDENT],
        pl.BlockSpec((slots, hidden), lambda i, *_: (0, 0)),
        struct((slots, hidden), bf16),
        [
            pltpu.VMEM((slots, width), bf16),
        ],
        prefetch=1,
    )(image_rows, vis_slot, own, other, slope, fc2_weight)


def merge_part(pre_grad, fc1_weight, part, parts):
    slots, _ = pre_grad.shape
    columns = fc1_weight.shape[0] // parts
    block = block_of(columns, 256)
    steps = columns // block

    def body(pre_ref, fc1_ref, out_ref):
        def step(i, carry):
            window = pl.ds(pl.multiple_of(i * block, LANES), block)
            rows = pl.ds(pl.multiple_of(part * columns + i * block, LANES), block)
            out_ref[:, window] = dot(pre_ref[...], fc1_ref[rows, :], 1, 1).astype(bf16)
            return carry

        lax.fori_loop(0, steps, step, 0)

    return run_kernel(
        body,
        (1,),
        [whole(pre_grad), RESIDENT],
        pl.BlockSpec((slots, columns), lambda i, *_: (0, 0)),
        struct((slots, columns), bf16),
    )(pre_grad, fc1_weight)


def project(own, other, gain, bias, weights, head_dim):
    patches, width = own.shape
    length = 2 * patches
    slots = length // 4
    sections, copies = len(weights), len(weights[0])
    part_rows, group_cols = weights[0][0].shape
    pieces = group_cols // head_dim
    flat = [w for parts in weights for w in parts]

    def body(own_ref, other_ref, gain_ref, bias_ref, *refs):
        w_refs, (out_ref, x, n) = refs[: len(flat)], refs[len(flat) :]
        section = lax.axis_index("section")
        put_rows(x, 0, own_ref[...].astype(f32))
        put_rows(x, patches, other_ref[...].astype(f32))
        gain, bias = gain_ref[...].reshape(1, width), bias_ref[...].reshape(1, width)
        for j in range(4):
            rows, _ = normalize(every_fourth(x, j, slots))
            rows = (rows * gain + bias).astype(bf16)
            for t in range(sections):
                n[t, j * slots : (j + 1) * slots, :] = rows[:, t * part_rows : (t + 1) * part_rows]
        for p in range(copies):
            total = sum(
                dot(n[section ^ k], w_refs[k * copies + p][:, :group_cols])
                for k in range(sections)
            ).T
            for c in range(pieces):
                out_ref[p, c] = total[c * head_dim : (c + 1) * head_dim].astype(bf16)

    shape = (copies, pieces, head_dim, length)
    return run_kernel(
        body,
        (1,),
        [whole(x) for x in (own, other, gain, bias, *flat)],
        pl.BlockSpec(shape, lambda i, *_: (0, 0, 0, 0)),
        struct(shape, bf16),
        [
            pltpu.VMEM((width // LANES, length, LANES), f32),
            pltpu.VMEM((sections, length, part_rows), bf16),
        ],
        limit=30,
    )(own, other, gain, bias, *flat)


def attention_back(
    image_rows, own, other, gain, mine, theirs, proj_weight, projected, weights, head_dim
):
    patches, width = own.shape
    length = 2 * patches
    slots = length // 4
    half = slots // 2
    images = image_rows.shape[0]
    sections, copies = len(weights), len(weights[0])
    part_rows, group_cols = weights[0][0].shape
    group_heads = group_cols // (3 * head_dim)
    part_heads = part_rows // head_dim
    shard_sections = copies * group_heads // part_heads
    flat = [w for parts in weights for w in parts]
    chunks = len(mine)
    per_chunk = 4 // chunks
    score_scale = head_dim ** (-0.5)

    def body(image_ref, own_ref, other_ref, gain_ref, *refs):
        gain = gain_ref[...].reshape(1, width)
        mine_refs, refs = refs[:chunks], refs[chunks:]
        theirs_refs, refs = refs[:chunks], refs[chunks:]
        proj_ref, projected_ref, refs = refs[0], refs[1], refs[2:]
        w_refs, refs = refs[: len(flat)], refs[len(flat) :]
        own_out, other_out, grad_out, x, og, og_parts, heads, acc = refs
        section, shard, copy = (lax.axis_index(name) for name in ("section", "vit", "dp"))
        ends = image_ends(image_ref, images)
        put_rows(x, 0, own_ref[...].astype(f32))
        put_rows(x, patches, other_ref[...].astype(f32))
        for j in range(4):
            rows, inverse = normalize(every_fourth(x, j, slots))
            cols = slice(j % per_chunk * width, (j % per_chunk + 1) * width)
            there = theirs_refs[j // per_chunk][:, cols]
            there = jnp.concatenate([there[half:], there[:half]], axis=0)
            upstream = mine_refs[j // per_chunk][:, cols].astype(f32) + there.astype(f32)
            result = normalize_back(upstream, rows, inverse, gain).astype(bf16)
            og[j * slots : (j + 1) * slots, :] = result
            grad_out[j] = result[:half]
            for t in range(sections):
                og_parts[t, j * slots : (j + 1) * slots, :] = result[
                    :, t * part_rows : (t + 1) * part_rows
                ]

        def put_heads(part, cols):
            for h in range(part_heads):
                heads[part * part_heads + h] = cols[h * head_dim : (h + 1) * head_dim].astype(bf16)

        for i in range(shard_sections):
            relation = section ^ (shard * shard_sections + i)
            for k in range(sections):

                @pl.when(relation == k)
                def _(i=i, k=k):
                    if k == 0:
                        put_heads(i, dot(proj_ref[...], og[...], 1, 1))
                    else:
                        fetched = [
                            w_refs[k * copies + p][:, group_cols : group_cols + part_rows]
                            for p in range(copies)
                        ]
                        put_heads(
                            i, sum(dot(w, og_parts[copy ^ p], 1, 1) for p, w in enumerate(fetched))
                        )

        def image_of(axis):
            index = lax.broadcasted_iota(jnp.int32, (length, length), axis) % slots
            position = ((index // half) ^ shard) * half + index % half
            image = jnp.zeros((length, length), jnp.int32)
            for e in range(images):
                image += (position >= ends[e]).astype(jnp.int32)
            return image

        image = image_of(0)
        allowed = (image == image_of(1)) & (image < images)
        dead = (image_of(1)[:1] == images).astype(f32)
        for p in range(copies):
            grads = [[], [], []]
            for h in range(group_heads):
                query, key, value = (projected_ref[p, c * group_heads + h] for c in range(3))
                grad = heads[(copy ^ p) * group_heads + h]
                scores = dot(key, query, 0, 0) * score_scale
                exponent = jnp.where(allowed, jnp.exp(scores), 0.0)
                denominator = jnp.sum(exponent, axis=0, keepdims=True) + dead
                softmax_weights = (exponent / denominator).astype(bf16)
                prob_grad = dot(value, grad, 0, 0)
                weighted = softmax_weights.astype(f32)
                row_dot = jnp.sum(weighted * prob_grad, axis=0, keepdims=True)
                score_grad = (weighted * (prob_grad - row_dot) * score_scale).astype(bf16)
                grads[0].append(dot(key, score_grad))
                grads[1].append(dot(query, score_grad, 1, 1))
                grads[2].append(dot(grad, softmax_weights, 1, 1))
            group_grad = jnp.concatenate([g for gs in grads for g in gs], axis=0).astype(bf16)
            for k in range(sections):
                term = dot(w_refs[k * copies + p][:, :group_cols], group_grad)
                acc[k] = term if p == 0 else acc[k] + term

        result = jnp.concatenate([acc[section ^ t] for t in range(sections)], axis=0).T
        for j in range(4):
            own_out[j] = result[j * slots : j * slots + half]
            other_out[j] = result[j * slots + half : (j + 1) * slots].astype(bf16)

    shape = (4, half, width)
    operands = (own, other, gain, *mine, *theirs, proj_weight, projected, *flat)
    return run_kernel(
        body,
        (1,),
        [whole(x) for x in operands],
        [pl.BlockSpec(shape, lambda i, *_: (0, 0, 0))] * 3,
        [struct(shape, f32), struct(shape, bf16), struct(shape, bf16)],
        [
            pltpu.VMEM((width // LANES, length, LANES), f32),
            pltpu.VMEM((length, width), bf16),
            pltpu.VMEM((sections, length, part_rows), bf16),
            pltpu.VMEM((copies * group_heads, head_dim, length), bf16),
            pltpu.VMEM((sections, part_rows, length), f32),
        ],
        prefetch=1,
        limit=40,
    )(image_rows, *operands)


def finish(own, gain, mine, theirs, out_grad):
    patches, width = own.shape

    def body(own_ref, gain_ref, mine_ref, theirs_ref, grad_ref, out_ref, x):
        gain = gain_ref[...].reshape(1, width)
        put_rows(x, 0, own_ref[...].astype(f32))
        for j in range(4):
            rows, inverse = normalize(every_fourth(x, j, patches // 4))
            upstream = mine_ref[j] + theirs_ref[j].astype(f32)
            result = grad_ref[j].astype(f32) + normalize_back(
                upstream, rows, inverse, gain
            )
            for c in range(x.shape[0]):
                x[c, pl.ds(j, patches // 4, stride=4), :] = result[:, c * LANES : (c + 1) * LANES]
        out_ref[...] = jnp.concatenate([x[c] for c in range(x.shape[0])], axis=1).astype(bf16)

    operands = (own, gain, mine, theirs, out_grad)
    return run_kernel(
        body,
        (1,),
        [whole(x) for x in operands],
        pl.BlockSpec((patches, width), lambda i, *_: (0, 0)),
        struct((patches, width), bf16),
        [pltpu.VMEM((width // LANES, patches, LANES), f32)],
    )(*operands)


def local_paired(
    grad_llm,
    vis_slot,
    image_rows,
    section_layer,
    vit_in,
    vit_out,
    ln_gain,
    ln_bias,
    qkv_weight,
    proj_weight,
    merge_gain,
    merge_bias,
    fc1_weight,
    fc1_bias,
    fc2_weight,
):
    sections = lax.axis_size("section")
    shards = lax.axis_size("vit")
    copies = lax.axis_size("dp")
    section_index = lax.axis_index("section")
    shard_index = lax.axis_index("vit")
    copy_index = lax.axis_index("dp")
    llm_width = grad_llm.shape[2]
    vit_width = vit_in.shape[1]
    head_dim = vit_width // HEADS
    part_rows = qkv_weight.shape[0]
    group_heads = HEADS // (shards * copies)
    group_rows = grad_llm.shape[1] // sections

    def own_group(p, source):
        first = (shard_index * copies + (copy_index ^ p)) * group_heads * head_dim
        return [
            lax.dynamic_slice_in_dim(source, c * vit_width + first, group_heads * head_dim, 1)
            for c in range(3)
        ]

    image_rows = image_rows.T

    outgoing = grad_llm[0].reshape(sections, group_rows, llm_width)
    arrived = {
        k: swap(
            lax.dynamic_index_in_dim(outgoing, section_index ^ k, 0, keepdims=False), "section", k
        )
        for k in range(1, sections)
    }
    vit_out_other = swap(vit_out, "vit", 1)
    proj_cols = lax.dynamic_slice_in_dim(proj_weight, copy_index * part_rows, part_rows, 1)
    own_parts = [jnp.concatenate(own_group(p, qkv_weight), axis=1) for p in range(copies)]
    piece = jnp.concatenate([own_parts[0], proj_cols], axis=1)
    near = swap(piece, "section", 1)
    far = swap(piece, "section", 2)
    vit_in_other = swap(vit_in, "vit", 1)
    slope = slope_of(vit_out, vit_out_other, merge_gain, merge_bias, fc1_weight, fc1_bias)
    arrived, slope = lax.optimization_barrier((arrived, slope))

    summed = weighted_sum(section_layer, grad_llm, [arrived[k] for k in range(1, sections)])
    summed_other = swap(summed, "vit", 1)
    near, summed = lax.optimization_barrier((near, summed))
    near_chip = swap(near, "dp", 2)
    near_core = swap(near, "dp", 1)

    pre_grad = pre_grad_of(image_rows, vis_slot, summed, summed_other, fc2_weight, slope)
    far, near_chip, pre_grad = lax.optimization_barrier((far, near_chip, pre_grad))
    cross = swap(far, "section", 1)
    far_chip = swap(far, "dp", 2)
    near_diagonal = swap(near_chip, "dp", 1)
    far_core = swap(far, "dp", 1)
    first = merge_part(pre_grad, fc1_weight, 0, 2)
    first_theirs = swap(first, "vit", 1)
    far_chip, pre_grad, first, cross = lax.optimization_barrier((far_chip, pre_grad, first, cross))
    cross_chip = swap(cross, "dp", 2)
    far_diagonal = swap(far_chip, "dp", 1)
    cross_core = swap(cross, "dp", 1)
    second = merge_part(pre_grad, fc1_weight, 1, 2)
    second_theirs = swap(second, "vit", 1)
    second, cross_chip = lax.optimization_barrier((second, cross_chip))
    cross_diagonal = swap(cross_chip, "dp", 1)
    weights = [
        own_parts,
        [near, near_core, near_chip, near_diagonal],
        [far, far_core, far_chip, far_diagonal],
        [cross, cross_core, cross_chip, cross_diagonal],
    ]

    projected = project(vit_in, vit_in_other, ln_gain, ln_bias, weights, head_dim)
    normed_mine, normed_sent, out_grad = attention_back(
        image_rows,
        vit_out,
        vit_out_other,
        merge_gain,
        [first, second],
        [first_theirs, second_theirs],
        proj_weight,
        projected,
        weights,
        head_dim,
    )
    normed_theirs = swap(normed_sent, "vit", 1)
    return finish(vit_in, ln_gain, normed_mine, normed_theirs, out_grad)


def solution(mesh):
    paired = fits(mesh)

    def chosen_form(*arguments):
        return (local_paired if paired else local)(*arguments)

    placed = (
        P("section", ("dp", "vit"), None),
        P("dp", None),
        P("dp", None),
        P(),
        P(("dp", "section", "vit"), None),
        P(("dp", "section", "vit"), None),
        P(),
        P(),
        P("section", None),
        P("section", None),
        P(),
        P(),
        P(None, "vit"),
        P("vit"),
        P("vit", None),
    )
    return jax.shard_map(
        chosen_form,
        mesh=mesh,
        in_specs=placed,
        out_specs=P(("dp", "section", "vit"), None),
        check_vma=False,
    )
```

```python
import jax
import jax.numpy as jnp
from jax import lax
from jax.experimental import pallas as pl
from jax.experimental.pallas import tpu as pltpu
from jax.sharding import PartitionSpec as P

HEADS = 16
LEVELS = 3


norm_eps = 1e-06


def normalize(values):
    row_mean = jnp.mean(values, axis=-1, keepdims=True)
    centered = values - row_mean
    variance = jnp.mean(centered * centered, axis=-1, keepdims=True)
    inverse = lax.rsqrt(variance + norm_eps)
    return (centered * inverse, inverse)


def normalize_back(upstream, normed_rows, inverse, gain):
    scaled = upstream * gain
    mean_scaled = jnp.mean(scaled, axis=-1, keepdims=True)
    mean_cross = jnp.mean(scaled * normed_rows, axis=-1, keepdims=True)
    return (scaled - mean_scaled - normed_rows * mean_cross) * inverse


def gelu_slope(pre_act):
    cumulative = 0.5 * (1.0 + lax.erf(pre_act * 0.7071067811865476))
    density = jnp.exp(-0.5 * pre_act * pre_act) * 0.3989422804014327
    return cumulative + pre_act * density


def local(
    grad_llm,
    vis_slot,
    image_rows,
    section_layer,
    vit_in,
    vit_out,
    ln_gain,
    ln_bias,
    qkv_weight,
    proj_weight,
    merge_gain,
    merge_bias,
    fc1_weight,
    fc1_bias,
    fc2_weight,
):
    sections = lax.axis_size("section")
    shards = lax.axis_size("vit")
    section_index = lax.axis_index("section")
    shard_index = lax.axis_index("vit")
    devices = sections * shards
    patches = vit_in.shape[0]
    slots_here = patches // 4
    run_rows = grad_llm.shape[1] // devices
    llm_width = grad_llm.shape[2]
    vit_width = vit_in.shape[1]
    head_dim = vit_width // HEADS
    device_index = section_index * shards + shard_index
    qkv_full, proj_full = (
        lax.all_gather(qkv_weight, "section", axis=0, tiled=True),
        lax.all_gather(proj_weight, "section", axis=0, tiled=True),
    )
    in_rows, in_inverse = normalize(vit_in.astype(jnp.float32))
    normed = (in_rows * ln_gain + ln_bias).astype(jnp.bfloat16)
    projected = lax.dot_general(
        qkv_full, normed, (((0,), (1,)), ((), ())), preferred_element_type=jnp.float32
    )
    projected = projected.astype(jnp.bfloat16).reshape(3, HEADS, head_dim, patches)
    section_weight = jnp.where(
        section_layer < LEVELS, (section_layer + 1).astype(jnp.float32) / LEVELS, 0.0
    )
    outgoing = grad_llm[0].reshape(devices, run_rows, llm_width)
    image_ends = jnp.cumsum(image_rows[section_index])
    out_rows, out_inverse = normalize(vit_out.astype(jnp.float32))
    merge_in = (
        (out_rows * merge_gain + merge_bias).astype(jnp.bfloat16).reshape(slots_here, 4 * vit_width)
    )
    arrived = lax.all_to_all(outgoing, ("section", "vit"), split_axis=0, concat_axis=0, tiled=True)
    arrived_f = arrived.reshape(sections, shards, run_rows, llm_width).astype(jnp.float32)
    incoming = jnp.sum(arrived_f * section_weight[:, None, None, None], axis=0)
    columns = lax.dynamic_slice_in_dim(vis_slot, device_index * run_rows, run_rows, 1)
    local_slot = (columns - device_index * slots_here).reshape(-1)
    placed = (
        jnp.zeros((slots_here, llm_width), jnp.float32)
        .at[local_slot]
        .set(incoming.reshape(-1, llm_width))
    )
    slot_position = shard_index * slots_here + jnp.arange(slots_here, dtype=jnp.int32)
    merged_grad = jnp.where((slot_position < image_ends[-1])[:, None], placed, 0.0).astype(
        jnp.bfloat16
    )
    rows_in, rows_grad = (
        lax.all_gather(merge_in, "vit", axis=0, tiled=True),
        lax.all_gather(merged_grad, "vit", axis=0, tiled=True),
    )
    pre_act = jnp.dot(rows_in, fc1_weight, preferred_element_type=jnp.float32) + fc1_bias
    hidden_grad = lax.dot_general(
        rows_grad, fc2_weight, (((1,), (1,)), ((), ())), preferred_element_type=jnp.float32
    )
    pre_grad = (hidden_grad * gelu_slope(pre_act)).astype(jnp.bfloat16)
    merge_grad = lax.psum_scatter(
        lax.dot_general(
            pre_grad, fc1_weight, (((1,), (1,)), ((), ())), preferred_element_type=jnp.float32
        ).astype(jnp.bfloat16),
        "vit",
        scatter_dimension=0,
        tiled=True,
    ).astype(jnp.float32)
    out_grad = normalize_back(
        merge_grad.reshape(patches, vit_width), out_rows, out_inverse, merge_gain
    ).astype(jnp.bfloat16)
    grad_cols = lax.dot_general(
        proj_full, out_grad, (((1,), (1,)), ((), ())), preferred_element_type=jnp.float32
    )
    grad_cols = grad_cols.astype(jnp.bfloat16).reshape(1, HEADS, head_dim, patches)
    head_inputs, head_grad = (
        lax.all_to_all(projected, "vit", split_axis=1, concat_axis=3, tiled=True),
        lax.all_to_all(grad_cols, "vit", split_axis=1, concat_axis=3, tiled=True),
    )
    length = shards * patches
    block_size = min(512, length)
    block_count = length // block_size
    slot_of = jnp.arange(length, dtype=jnp.int32) // 4
    patch_image = jnp.sum((slot_of[:, None] >= image_ends[None, :]).astype(jnp.int32), axis=1)
    patch_live = slot_of < image_ends[-1]
    score_scale = head_dim ** (-0.5)
    contract_first = (((0,), (0,)), ((), ()))

    def head_backward(query_cols, key_cols, value_cols, grad_head):

        def step(carry, block_index):
            key_acc, value_acc = carry
            first_row = block_index * block_size
            query_block = lax.dynamic_slice_in_dim(query_cols, first_row, block_size, 1)
            grad_block = lax.dynamic_slice_in_dim(grad_head, first_row, block_size, 1)
            image_block = lax.dynamic_slice_in_dim(patch_image, first_row, block_size, 0)
            live_block = lax.dynamic_slice_in_dim(patch_live, first_row, block_size, 0)
            scores = (
                lax.dot_general(
                    query_block, key_cols, contract_first, preferred_element_type=jnp.float32
                )
                * score_scale
            )
            allowed = (
                (image_block[:, None] == patch_image[None, :])
                & live_block[:, None]
                & patch_live[None, :]
            )
            exponent = jnp.where(allowed, jnp.exp(jnp.where(allowed, scores, 0.0)), 0.0)
            denominator = (
                jnp.sum(exponent, axis=1, keepdims=True)
                + 1.0
                - live_block.astype(jnp.float32)[:, None]
            )
            softmax_weights = (exponent / denominator).astype(jnp.bfloat16)
            prob_grad = lax.dot_general(
                grad_block, value_cols, contract_first, preferred_element_type=jnp.float32
            )
            weighted = softmax_weights.astype(jnp.float32)
            row_dot = jnp.sum(weighted * prob_grad, axis=1, keepdims=True)
            score_grad = (weighted * (prob_grad - row_dot) * score_scale).astype(jnp.bfloat16)
            query_grad = lax.dot_general(
                key_cols, score_grad, (((1,), (1,)), ((), ())), preferred_element_type=jnp.float32
            )
            key_acc = key_acc + lax.dot_general(
                query_block,
                score_grad,
                (((1,), (0,)), ((), ())),
                preferred_element_type=jnp.float32,
            )
            value_acc = value_acc + lax.dot_general(
                grad_block,
                softmax_weights,
                (((1,), (0,)), ((), ())),
                preferred_element_type=jnp.float32,
            )
            return ((key_acc, value_acc), query_grad.astype(jnp.bfloat16))

        empty = jnp.zeros((head_dim, length), jnp.float32)
        (key_total, value_total), query_blocks = lax.scan(
            step, (empty, empty), jnp.arange(block_count, dtype=jnp.int32)
        )
        query_total = query_blocks.transpose(1, 0, 2).reshape(head_dim, length)
        return (query_total, key_total.astype(jnp.bfloat16), value_total.astype(jnp.bfloat16))

    query_all, key_all, value_all = jax.vmap(head_backward)(
        head_inputs[0], head_inputs[1], head_inputs[2], head_grad[0]
    )
    head_result = jnp.stack([query_all, key_all, value_all])
    returned = lax.all_to_all(head_result, "vit", split_axis=3, concat_axis=1, tiled=True)
    projected_grad = returned.reshape(3 * vit_width, patches)
    normed_grad = lax.dot_general(
        projected_grad, qkv_full, (((0,), (1,)), ((), ())), preferred_element_type=jnp.float32
    )
    vit_grad = out_grad.astype(jnp.float32) + normalize_back(
        normed_grad, in_rows, in_inverse, ln_gain
    )
    return vit_grad.astype(jnp.bfloat16)


bf16, f32 = jnp.bfloat16, jnp.float32


def swap(values, axis, bit):
    count = lax.axis_size(axis)
    return lax.ppermute(values, axis, [(i, i ^ bit) for i in range(count)])


def fits(mesh):
    sections, copies, shards = (mesh.shape[name] for name in ("section", "dp", "vit"))
    return (sections, copies, shards) == (4, 4, 2)


def dot(a, b, ca=1, cb=0):
    return lax.dot_general(a, b, (((ca,), (cb,)), ((), ())), preferred_element_type=f32)


def block_of(size, limit):
    return max(b for b in range(128, limit + 1, 128) if size % b == 0)


def run_kernel(body, grid, in_specs, out_specs, out_shape, scratch=(), prefetch=0, limit=10, cost=0):
    return pl.pallas_call(
        body,
        grid_spec=pltpu.PrefetchScalarGridSpec(
            num_scalar_prefetch=prefetch,
            grid=grid,
            in_specs=in_specs,
            out_specs=out_specs,
            scratch_shapes=list(scratch),
        ),
        out_shape=out_shape,
        cost_estimate=pl.CostEstimate(flops=cost, transcendentals=0, bytes_accessed=0)
        if cost
        else None,
        compiler_params=pltpu.CompilerParams(
            dimension_semantics=("arbitrary",) * len(grid), vmem_limit_bytes=limit << 20
        ),
    )


def whole(array):
    return pl.BlockSpec(array.shape, lambda i, *_: (0,) * array.ndim)


RESIDENT = pl.BlockSpec(memory_space=pltpu.VMEM)


def struct(shape, dtype):
    return jax.ShapeDtypeStruct(shape, dtype)


LANES = 128
COST = 8_000_000_000


def put_rows(ref, first, values):
    for c in range(ref.shape[0]):
        ref[c, first : first + values.shape[0], :] = values[:, c * LANES : (c + 1) * LANES]


def every_fourth(ref, j, count):
    return jnp.concatenate(
        [ref[c, pl.ds(j, count, stride=4), :] for c in range(ref.shape[0])], axis=1
    )


def image_ends(image_ref, images):
    group, ends = lax.axis_index("section"), []
    for k in range(images):
        ends.append(image_ref[k, group] + (ends[-1] if ends else 0))
    return ends


def weighted_sum(section_layer, grad_llm, arrived):
    rows, width = arrived[0].shape

    def body(layer_ref, grad_ref, *refs):
        arrived_refs, (out_ref, own, sem) = refs[:-3], refs[-3:]
        here = lax.axis_index("section")
        window = pl.ds(pl.multiple_of(here * rows, 16), rows)
        copy = pltpu.make_async_copy(grad_ref.at[0, window, :], own, sem)
        copy.start()

        def term(section, values):
            layer = layer_ref[section]
            weight = jnp.where(layer < LEVELS, (layer + 1).astype(f32) / LEVELS, 0.0)
            return weight * values.astype(f32)

        total = sum(term(here ^ (k + 1), ref[...]) for k, ref in enumerate(arrived_refs))
        copy.wait()
        out_ref[...] = (total + term(here, own[...])).astype(bf16)

    return run_kernel(
        body,
        (1,),
        [pl.BlockSpec(memory_space=pl.ANY)] + [whole(x) for x in arrived],
        pl.BlockSpec((rows, width), lambda i, *_: (0, 0)),
        struct((rows, width), bf16),
        [pltpu.VMEM((rows, width), bf16), pltpu.SemaphoreType.DMA],
        prefetch=1,
        limit=4,
    )(section_layer, grad_llm, *arrived)


def own_columns(qkv_weight, proj_weight, shards, copies):
    part_rows, width = proj_weight.shape
    group = qkv_weight.shape[1] // (3 * shards * copies)

    def body(qkv_ref, proj_ref, piece_ref, *part_refs):
        place = lax.axis_index("vit") * copies + lax.axis_index("dp")
        for v in range(shards):
            for q in range(copies):

                @pl.when(place == v * copies + q)
                def _(v=v, q=q):
                    for p in range(copies):
                        first = (v * copies + (q ^ p)) * group
                        cols = jnp.concatenate(
                            [qkv_ref[:, c * width + first : c * width + first + group] for c in range(3)],
                            axis=1,
                        )
                        part_refs[p][...] = cols
                        if p == 0:
                            columns = proj_ref[:, q * part_rows : (q + 1) * part_rows]
                            piece_ref[...] = jnp.concatenate([cols, columns], axis=1)

    shapes = [(part_rows, 3 * group + part_rows)] + [(part_rows, 3 * group)] * copies
    return run_kernel(
        body,
        (1,),
        [whole(qkv_weight), whole(proj_weight)],
        [pl.BlockSpec(shape, lambda i, *_: (0, 0)) for shape in shapes],
        [struct(shape, bf16) for shape in shapes],
        limit=16,
        cost=COST,
    )(qkv_weight, proj_weight)


def slope_of(own, other, gain, bias, fc1_weight, fc1_bias):
    patches, width = own.shape
    slots = patches * 2 // 4
    depth, hidden = fc1_weight.shape
    block = block_of(hidden, 256)
    steps = hidden // block

    def body(own_ref, other_ref, gain_ref, bias_ref, fc1b_ref, fc1_ref, out_ref, x, m):
        put_rows(x, 0, own_ref[...].astype(f32))
        put_rows(x, patches, other_ref[...].astype(f32))
        gain, bias = gain_ref[...].reshape(1, width), bias_ref[...].reshape(1, width)
        for j in range(4):
            rows, _ = normalize(every_fourth(x, j, slots))
            m[:, j * width : (j + 1) * width] = (rows * gain + bias).astype(bf16)

        def step(i, carry):
            window = pl.ds(pl.multiple_of(i * block, LANES), block)
            pre_act = dot(m[...], fc1_ref[:, window]) + fc1b_ref[window].reshape(1, block)
            out_ref[:, window] = gelu_slope(pre_act)
            return carry

        lax.fori_loop(0, steps, step, 0)

    return run_kernel(
        body,
        (1,),
        [whole(x) for x in (own, other, gain, bias, fc1_bias)]
        + [RESIDENT],
        pl.BlockSpec((slots, hidden), lambda i, *_: (0, 0)),
        struct((slots, hidden), f32),
        [
            pltpu.VMEM((width // LANES, 2 * patches, LANES), f32),
            pltpu.VMEM((slots, depth), bf16),
        ],
        cost=COST,
        limit=5,
    )(own, other, gain, bias, fc1_bias, fc1_weight)


def pre_grad_of(image_rows, vis_slot, own, other, fc2_weight, slope):
    rows, width = own.shape
    slots, hidden = slope.shape
    half = slots // 2
    llm_rows = vis_slot.shape[1]
    images = image_rows.shape[0]
    block = block_of(hidden, 256)
    steps = hidden // block

    def body(
        image_ref, slot_ref, own_ref, other_ref, slope_ref, fc2_ref, out_ref, merged, buffer, sems
    ):
        def fetch(i):
            rows_here = pl.ds(pl.multiple_of(i * block, LANES), block)
            return pltpu.make_async_copy(fc2_ref.at[rows_here, :], buffer.at[i], sems.at[i])

        for i in range(steps):
            fetch(i).start()
        section, shard = lax.axis_index("section"), lax.axis_index("vit")
        index = lax.broadcasted_iota(jnp.int32, (slots, llm_rows), 0)
        position = ((index // half) ^ shard) * half + index % half
        live = position < image_ends(image_ref, images)[-1]
        shift = (
            lax.broadcasted_iota(jnp.int32, (llm_rows, rows), 0)
            == lax.broadcasted_iota(jnp.int32, (llm_rows, rows), 1) + section * rows
        ).astype(bf16)
        chosen = []
        for part in range(2):
            named = slot_ref[pl.ds(shard ^ part, 1), :] - section * slots
            found = ((position == named) & live).astype(f32).astype(bf16)
            chosen.append(dot(found, shift))
        chosen = jnp.concatenate(chosen, axis=1).astype(bf16)
        total = dot(chosen, jnp.concatenate([own_ref[...], other_ref[...]], axis=0))
        merged[...] = total.astype(bf16)

        def step(i, carry):
            window = pl.ds(pl.multiple_of(i * block, LANES), block)
            fetch(i).wait()
            hidden_grad = dot(merged[...], buffer[i], 1, 1)
            out_ref[:, window] = (hidden_grad * slope_ref[:, window]).astype(bf16)
            return carry

        lax.fori_loop(0, steps, step, 0)

    return run_kernel(
        body,
        (1,),
        [whole(x) for x in (vis_slot, own, other, slope)] + [pl.BlockSpec(memory_space=pltpu.HBM)],
        pl.BlockSpec((slots, hidden), lambda i, *_: (0, 0)),
        struct((slots, hidden), bf16),
        [
            pltpu.VMEM((slots, width), bf16),
            pltpu.VMEM((steps, block, width), bf16),
            pltpu.SemaphoreType.DMA((steps,)),
        ],
        prefetch=1,
        limit=22,
    )(
        image_rows,
        vis_slot,
        own,
        other,
        slope,
        pltpu.with_memory_space_constraint(fc2_weight, pltpu.HBM),
    )


def merge_part(pre_grad, fc1_weight, part, parts):
    slots, _ = pre_grad.shape
    columns = fc1_weight.shape[0] // parts
    block = block_of(columns, 256)
    steps = columns // block

    def body(pre_ref, fc1_ref, out_ref):
        def step(i, carry):
            window = pl.ds(pl.multiple_of(i * block, LANES), block)
            rows = pl.ds(pl.multiple_of(part * columns + i * block, LANES), block)
            out_ref[:, window] = dot(pre_ref[...], fc1_ref[rows, :], 1, 1).astype(bf16)
            return carry

        lax.fori_loop(0, steps, step, 0)

    return run_kernel(
        body,
        (1,),
        [whole(pre_grad), RESIDENT],
        pl.BlockSpec((slots, columns), lambda i, *_: (0, 0)),
        struct((slots, columns), bf16),
        limit=2,
    )(pre_grad, fc1_weight)


def project(own, other, gain, bias, weights, head_dim):
    patches, width = own.shape
    length = 2 * patches
    slots = length // 4
    sections, copies = len(weights), len(weights[0])
    part_rows, group_cols = weights[0][0].shape
    pieces = group_cols // head_dim
    flat = [w for parts in weights for w in parts]

    def body(own_ref, other_ref, gain_ref, bias_ref, *refs):
        w_refs, (out_ref, x, n) = refs[: len(flat)], refs[len(flat) :]
        section = lax.axis_index("section")
        put_rows(x, 0, own_ref[...].astype(f32))
        put_rows(x, patches, other_ref[...].astype(f32))
        gain, bias = gain_ref[...].reshape(1, width), bias_ref[...].reshape(1, width)
        for j in range(4):
            rows, _ = normalize(every_fourth(x, j, slots))
            rows = (rows * gain + bias).astype(bf16)
            for t in range(sections):
                n[t, j * slots : (j + 1) * slots, :] = rows[:, t * part_rows : (t + 1) * part_rows]
        for p in range(copies):
            total = sum(
                dot(n[section ^ k], w_refs[k * copies + p][:, :group_cols])
                for k in range(sections)
            ).T
            for c in range(pieces):
                out_ref[p, c] = total[c * head_dim : (c + 1) * head_dim].astype(bf16)

    shape = (copies, pieces, head_dim, length)
    return run_kernel(
        body,
        (1,),
        [whole(x) for x in (own, other, gain, bias, *flat)],
        pl.BlockSpec(shape, lambda i, *_: (0, 0, 0, 0)),
        struct(shape, bf16),
        [
            pltpu.VMEM((width // LANES, length, LANES), f32),
            pltpu.VMEM((sections, length, part_rows), bf16),
        ],
        limit=30,
    )(own, other, gain, bias, *flat)


def attention_back(
    image_rows, own, other, gain, mine, theirs, proj_weight, projected, weights, head_dim
):
    patches, width = own.shape
    length = 2 * patches
    slots = length // 4
    half = slots // 2
    images = image_rows.shape[0]
    sections, copies = len(weights), len(weights[0])
    part_rows, group_cols = weights[0][0].shape
    group_heads = group_cols // (3 * head_dim)
    part_heads = part_rows // head_dim
    shard_sections = copies * group_heads // part_heads
    flat = [w for parts in weights for w in parts]
    chunks = len(mine)
    per_chunk = 4 // chunks
    score_scale = head_dim ** (-0.5)

    def body(image_ref, own_ref, other_ref, gain_ref, *refs):
        gain = gain_ref[...].reshape(1, width)
        mine_refs, refs = refs[:chunks], refs[chunks:]
        theirs_refs, refs = refs[:chunks], refs[chunks:]
        proj_ref, projected_ref, refs = refs[0], refs[1], refs[2:]
        w_refs, refs = refs[: len(flat)], refs[len(flat) :]
        own_out, other_out, grad_out, x, og, og_parts, heads, acc = refs
        section, shard, copy = (lax.axis_index(name) for name in ("section", "vit", "dp"))
        ends = image_ends(image_ref, images)
        put_rows(x, 0, own_ref[...].astype(f32))
        put_rows(x, patches, other_ref[...].astype(f32))
        for j in range(4):
            rows, inverse = normalize(every_fourth(x, j, slots))
            cols = slice(j % per_chunk * width, (j % per_chunk + 1) * width)
            there = theirs_refs[j // per_chunk][:, cols]
            there = jnp.concatenate([there[half:], there[:half]], axis=0)
            upstream = mine_refs[j // per_chunk][:, cols].astype(f32) + there.astype(f32)
            result = normalize_back(upstream, rows, inverse, gain).astype(bf16)
            og[j * slots : (j + 1) * slots, :] = result
            grad_out[j] = result[:half]
            for t in range(sections):
                og_parts[t, j * slots : (j + 1) * slots, :] = result[
                    :, t * part_rows : (t + 1) * part_rows
                ]

        def put_heads(part, cols):
            for h in range(part_heads):
                heads[part * part_heads + h] = cols[h * head_dim : (h + 1) * head_dim].astype(bf16)

        for i in range(shard_sections):
            relation = section ^ (shard * shard_sections + i)
            for k in range(sections):

                @pl.when(relation == k)
                def _(i=i, k=k):
                    if k == 0:
                        put_heads(i, dot(proj_ref[...], og[...], 1, 1))
                    else:
                        fetched = [
                            w_refs[k * copies + p][:, group_cols : group_cols + part_rows]
                            for p in range(copies)
                        ]
                        put_heads(
                            i, sum(dot(w, og_parts[copy ^ p], 1, 1) for p, w in enumerate(fetched))
                        )

        def image_of(axis):
            index = lax.broadcasted_iota(jnp.int32, (length, length), axis) % slots
            position = ((index // half) ^ shard) * half + index % half
            image = jnp.zeros((length, length), jnp.int32)
            for e in range(images):
                image += (position >= ends[e]).astype(jnp.int32)
            return image

        image = image_of(0)
        allowed = (image == image_of(1)) & (image < images)
        dead = (image_of(1)[:1] == images).astype(f32)
        for p in range(copies):
            grads = [[], [], []]
            for h in range(group_heads):
                query, key, value = (projected_ref[p, c * group_heads + h] for c in range(3))
                grad = heads[(copy ^ p) * group_heads + h]
                scores = dot(key, query, 0, 0) * score_scale
                exponent = jnp.where(allowed, jnp.exp(scores), 0.0)
                denominator = jnp.sum(exponent, axis=0, keepdims=True) + dead
                softmax_weights = (exponent / denominator).astype(bf16)
                prob_grad = dot(value, grad, 0, 0)
                weighted = softmax_weights.astype(f32)
                row_dot = jnp.sum(weighted * prob_grad, axis=0, keepdims=True)
                score_grad = (weighted * (prob_grad - row_dot) * score_scale).astype(bf16)
                grads[0].append(dot(key, score_grad))
                grads[1].append(dot(query, score_grad, 1, 1))
                grads[2].append(dot(grad, softmax_weights, 1, 1))
            group_grad = jnp.concatenate([g for gs in grads for g in gs], axis=0).astype(bf16)
            for k in range(sections):
                term = dot(w_refs[k * copies + p][:, :group_cols], group_grad)
                acc[k] = term if p == 0 else acc[k] + term

        result = jnp.concatenate([acc[section ^ t] for t in range(sections)], axis=0).T
        for j in range(4):
            own_out[j] = result[j * slots : j * slots + half]
            other_out[j] = result[j * slots + half : (j + 1) * slots].astype(bf16)

    shape = (4, half, width)
    operands = (own, other, gain, *mine, *theirs, proj_weight, projected, *flat)
    return run_kernel(
        body,
        (1,),
        [whole(x) for x in operands],
        [pl.BlockSpec(shape, lambda i, *_: (0, 0, 0))] * 3,
        [struct(shape, f32), struct(shape, bf16), struct(shape, bf16)],
        [
            pltpu.VMEM((width // LANES, length, LANES), f32),
            pltpu.VMEM((length, width), bf16),
            pltpu.VMEM((sections, length, part_rows), bf16),
            pltpu.VMEM((copies * group_heads, head_dim, length), bf16),
            pltpu.VMEM((sections, part_rows, length), f32),
        ],
        prefetch=1,
        limit=40,
    )(image_rows, *operands)


def finish(own, gain, mine, theirs, out_grad):
    patches, width = own.shape

    def body(own_ref, gain_ref, mine_ref, theirs_ref, grad_ref, out_ref, x):
        gain = gain_ref[...].reshape(1, width)
        put_rows(x, 0, own_ref[...].astype(f32))
        for j in range(4):
            rows, inverse = normalize(every_fourth(x, j, patches // 4))
            upstream = mine_ref[j] + theirs_ref[j].astype(f32)
            result = grad_ref[j].astype(f32) + normalize_back(
                upstream, rows, inverse, gain
            )
            for c in range(x.shape[0]):
                x[c, pl.ds(j, patches // 4, stride=4), :] = result[:, c * LANES : (c + 1) * LANES]
        out_ref[...] = jnp.concatenate([x[c] for c in range(x.shape[0])], axis=1).astype(bf16)

    operands = (own, gain, mine, theirs, out_grad)
    return run_kernel(
        body,
        (1,),
        [whole(x) for x in operands],
        pl.BlockSpec((patches, width), lambda i, *_: (0, 0)),
        struct((patches, width), bf16),
        [pltpu.VMEM((width // LANES, patches, LANES), f32)],
    )(*operands)


def local_paired(
    grad_llm,
    vis_slot,
    image_rows,
    section_layer,
    vit_in,
    vit_out,
    ln_gain,
    ln_bias,
    qkv_weight,
    proj_weight,
    merge_gain,
    merge_bias,
    fc1_weight,
    fc1_bias,
    fc2_weight,
):
    sections = lax.axis_size("section")
    shards = lax.axis_size("vit")
    copies = lax.axis_size("dp")
    section_index = lax.axis_index("section")
    llm_width = grad_llm.shape[2]
    vit_width = vit_in.shape[1]
    head_dim = vit_width // HEADS
    group_rows = grad_llm.shape[1] // sections
    image_rows = image_rows.T

    outgoing = grad_llm[0].reshape(sections, group_rows, llm_width)
    arrived = {
        k: swap(
            lax.dynamic_index_in_dim(outgoing, section_index ^ k, 0, keepdims=False), "section", k
        )
        for k in range(1, sections)
    }
    vit_out_other = swap(vit_out, "vit", 1)
    piece, *own_parts = own_columns(qkv_weight, proj_weight, shards, copies)
    near = swap(piece, "section", 1)
    far = swap(piece, "section", 2)
    vit_in_other = swap(vit_in, "vit", 1)
    slope = slope_of(vit_out, vit_out_other, merge_gain, merge_bias, fc1_weight, fc1_bias)
    arrived, slope = lax.optimization_barrier((arrived, slope))

    summed = weighted_sum(section_layer, grad_llm, [arrived[k] for k in range(1, sections)])
    summed_other = swap(summed, "vit", 1)
    near, summed_other = lax.optimization_barrier((near, summed_other))
    near_chip = swap(near, "dp", 2)
    near_core = swap(near, "dp", 1)

    pre_grad = pre_grad_of(image_rows, vis_slot, summed, summed_other, fc2_weight, slope)
    far, near_chip, pre_grad = lax.optimization_barrier((far, near_chip, pre_grad))
    cross = swap(far, "section", 1)
    far_chip = swap(far, "dp", 2)
    near_diagonal = swap(near_chip, "dp", 1)
    far_core = swap(far, "dp", 1)
    first = merge_part(pre_grad, fc1_weight, 0, 2)
    first_theirs = swap(first, "vit", 1)
    far_chip, pre_grad, first, cross = lax.optimization_barrier((far_chip, pre_grad, first, cross))
    cross_chip = swap(cross, "dp", 2)
    far_diagonal = swap(far_chip, "dp", 1)
    cross_core = swap(cross, "dp", 1)
    second = merge_part(pre_grad, fc1_weight, 1, 2)
    second_theirs = swap(second, "vit", 1)
    second, cross_chip = lax.optimization_barrier((second, cross_chip))
    cross_diagonal = swap(cross_chip, "dp", 1)
    weights = [
        own_parts,
        [near, near_core, near_chip, near_diagonal],
        [far, far_core, far_chip, far_diagonal],
        [cross, cross_core, cross_chip, cross_diagonal],
    ]

    projected = project(vit_in, vit_in_other, ln_gain, ln_bias, weights, head_dim)
    normed_mine, normed_sent, out_grad = attention_back(
        image_rows,
        vit_out,
        vit_out_other,
        merge_gain,
        [first, second],
        [first_theirs, second_theirs],
        proj_weight,
        projected,
        weights,
        head_dim,
    )
    normed_theirs = swap(normed_sent, "vit", 1)
    return finish(vit_in, ln_gain, normed_mine, normed_theirs, out_grad)


def solution(mesh):
    paired = fits(mesh)

    def chosen_form(*arguments):
        return (local_paired if paired else local)(*arguments)

    placed = (
        P("section", ("dp", "vit"), None),
        P("dp", None),
        P("dp", None),
        P(),
        P(("dp", "section", "vit"), None),
        P(("dp", "section", "vit"), None),
        P(),
        P(),
        P("section", None),
        P("section", None),
        P(),
        P(),
        P(None, "vit"),
        P("vit"),
        P("vit", None),
    )
    return jax.shard_map(
        chosen_form,
        mesh=mesh,
        in_specs=placed,
        out_specs=P(("dp", "section", "vit"), None),
        check_vma=False,
    )
```

```python
import jax
import jax.numpy as jnp
from jax import lax
from jax.experimental import pallas as pl
from jax.experimental.pallas import tpu as pltpu
from jax.sharding import PartitionSpec as P

HEADS = 16
LEVELS = 3


norm_eps = 1e-06


def normalize(values):
    row_mean = jnp.mean(values, axis=-1, keepdims=True)
    centered = values - row_mean
    variance = jnp.mean(centered * centered, axis=-1, keepdims=True)
    inverse = lax.rsqrt(variance + norm_eps)
    return (centered * inverse, inverse)


def normalize_back(upstream, normed_rows, inverse, gain):
    scaled = upstream * gain
    mean_scaled = jnp.mean(scaled, axis=-1, keepdims=True)
    mean_cross = jnp.mean(scaled * normed_rows, axis=-1, keepdims=True)
    return (scaled - mean_scaled - normed_rows * mean_cross) * inverse


def gelu_slope(pre_act):
    cumulative = 0.5 * (1.0 + lax.erf(pre_act * 0.7071067811865476))
    density = jnp.exp(-0.5 * pre_act * pre_act) * 0.3989422804014327
    return cumulative + pre_act * density


def local(
    grad_llm,
    vis_slot,
    image_rows,
    section_layer,
    vit_in,
    vit_out,
    ln_gain,
    ln_bias,
    qkv_weight,
    proj_weight,
    merge_gain,
    merge_bias,
    fc1_weight,
    fc1_bias,
    fc2_weight,
):
    sections = lax.axis_size("section")
    shards = lax.axis_size("vit")
    section_index = lax.axis_index("section")
    shard_index = lax.axis_index("vit")
    devices = sections * shards
    patches = vit_in.shape[0]
    slots_here = patches // 4
    run_rows = grad_llm.shape[1] // devices
    llm_width = grad_llm.shape[2]
    vit_width = vit_in.shape[1]
    head_dim = vit_width // HEADS
    device_index = section_index * shards + shard_index
    qkv_full, proj_full = (
        lax.all_gather(qkv_weight, "section", axis=0, tiled=True),
        lax.all_gather(proj_weight, "section", axis=0, tiled=True),
    )
    in_rows, in_inverse = normalize(vit_in.astype(jnp.float32))
    normed = (in_rows * ln_gain + ln_bias).astype(jnp.bfloat16)
    projected = lax.dot_general(
        qkv_full, normed, (((0,), (1,)), ((), ())), preferred_element_type=jnp.float32
    )
    projected = projected.astype(jnp.bfloat16).reshape(3, HEADS, head_dim, patches)
    section_weight = jnp.where(
        section_layer < LEVELS, (section_layer + 1).astype(jnp.float32) / LEVELS, 0.0
    )
    outgoing = grad_llm[0].reshape(devices, run_rows, llm_width)
    image_ends = jnp.cumsum(image_rows[section_index])
    out_rows, out_inverse = normalize(vit_out.astype(jnp.float32))
    merge_in = (
        (out_rows * merge_gain + merge_bias).astype(jnp.bfloat16).reshape(slots_here, 4 * vit_width)
    )
    arrived = lax.all_to_all(outgoing, ("section", "vit"), split_axis=0, concat_axis=0, tiled=True)
    arrived_f = arrived.reshape(sections, shards, run_rows, llm_width).astype(jnp.float32)
    incoming = jnp.sum(arrived_f * section_weight[:, None, None, None], axis=0)
    columns = lax.dynamic_slice_in_dim(vis_slot, device_index * run_rows, run_rows, 1)
    local_slot = (columns - device_index * slots_here).reshape(-1)
    placed = (
        jnp.zeros((slots_here, llm_width), jnp.float32)
        .at[local_slot]
        .set(incoming.reshape(-1, llm_width))
    )
    slot_position = shard_index * slots_here + jnp.arange(slots_here, dtype=jnp.int32)
    merged_grad = jnp.where((slot_position < image_ends[-1])[:, None], placed, 0.0).astype(
        jnp.bfloat16
    )
    rows_in, rows_grad = (
        lax.all_gather(merge_in, "vit", axis=0, tiled=True),
        lax.all_gather(merged_grad, "vit", axis=0, tiled=True),
    )
    pre_act = jnp.dot(rows_in, fc1_weight, preferred_element_type=jnp.float32) + fc1_bias
    hidden_grad = lax.dot_general(
        rows_grad, fc2_weight, (((1,), (1,)), ((), ())), preferred_element_type=jnp.float32
    )
    pre_grad = (hidden_grad * gelu_slope(pre_act)).astype(jnp.bfloat16)
    merge_grad = lax.psum_scatter(
        lax.dot_general(
            pre_grad, fc1_weight, (((1,), (1,)), ((), ())), preferred_element_type=jnp.float32
        ).astype(jnp.bfloat16),
        "vit",
        scatter_dimension=0,
        tiled=True,
    ).astype(jnp.float32)
    out_grad = normalize_back(
        merge_grad.reshape(patches, vit_width), out_rows, out_inverse, merge_gain
    ).astype(jnp.bfloat16)
    grad_cols = lax.dot_general(
        proj_full, out_grad, (((1,), (1,)), ((), ())), preferred_element_type=jnp.float32
    )
    grad_cols = grad_cols.astype(jnp.bfloat16).reshape(1, HEADS, head_dim, patches)
    head_inputs, head_grad = (
        lax.all_to_all(projected, "vit", split_axis=1, concat_axis=3, tiled=True),
        lax.all_to_all(grad_cols, "vit", split_axis=1, concat_axis=3, tiled=True),
    )
    length = shards * patches
    block_size = min(512, length)
    block_count = length // block_size
    slot_of = jnp.arange(length, dtype=jnp.int32) // 4
    patch_image = jnp.sum((slot_of[:, None] >= image_ends[None, :]).astype(jnp.int32), axis=1)
    patch_live = slot_of < image_ends[-1]
    score_scale = head_dim ** (-0.5)
    contract_first = (((0,), (0,)), ((), ()))

    def head_backward(query_cols, key_cols, value_cols, grad_head):

        def step(carry, block_index):
            key_acc, value_acc = carry
            first_row = block_index * block_size
            query_block = lax.dynamic_slice_in_dim(query_cols, first_row, block_size, 1)
            grad_block = lax.dynamic_slice_in_dim(grad_head, first_row, block_size, 1)
            image_block = lax.dynamic_slice_in_dim(patch_image, first_row, block_size, 0)
            live_block = lax.dynamic_slice_in_dim(patch_live, first_row, block_size, 0)
            scores = (
                lax.dot_general(
                    query_block, key_cols, contract_first, preferred_element_type=jnp.float32
                )
                * score_scale
            )
            allowed = (
                (image_block[:, None] == patch_image[None, :])
                & live_block[:, None]
                & patch_live[None, :]
            )
            exponent = jnp.where(allowed, jnp.exp(jnp.where(allowed, scores, 0.0)), 0.0)
            denominator = (
                jnp.sum(exponent, axis=1, keepdims=True)
                + 1.0
                - live_block.astype(jnp.float32)[:, None]
            )
            softmax_weights = (exponent / denominator).astype(jnp.bfloat16)
            prob_grad = lax.dot_general(
                grad_block, value_cols, contract_first, preferred_element_type=jnp.float32
            )
            weighted = softmax_weights.astype(jnp.float32)
            row_dot = jnp.sum(weighted * prob_grad, axis=1, keepdims=True)
            score_grad = (weighted * (prob_grad - row_dot) * score_scale).astype(jnp.bfloat16)
            query_grad = lax.dot_general(
                key_cols, score_grad, (((1,), (1,)), ((), ())), preferred_element_type=jnp.float32
            )
            key_acc = key_acc + lax.dot_general(
                query_block,
                score_grad,
                (((1,), (0,)), ((), ())),
                preferred_element_type=jnp.float32,
            )
            value_acc = value_acc + lax.dot_general(
                grad_block,
                softmax_weights,
                (((1,), (0,)), ((), ())),
                preferred_element_type=jnp.float32,
            )
            return ((key_acc, value_acc), query_grad.astype(jnp.bfloat16))

        empty = jnp.zeros((head_dim, length), jnp.float32)
        (key_total, value_total), query_blocks = lax.scan(
            step, (empty, empty), jnp.arange(block_count, dtype=jnp.int32)
        )
        query_total = query_blocks.transpose(1, 0, 2).reshape(head_dim, length)
        return (query_total, key_total.astype(jnp.bfloat16), value_total.astype(jnp.bfloat16))

    query_all, key_all, value_all = jax.vmap(head_backward)(
        head_inputs[0], head_inputs[1], head_inputs[2], head_grad[0]
    )
    head_result = jnp.stack([query_all, key_all, value_all])
    returned = lax.all_to_all(head_result, "vit", split_axis=3, concat_axis=1, tiled=True)
    projected_grad = returned.reshape(3 * vit_width, patches)
    normed_grad = lax.dot_general(
        projected_grad, qkv_full, (((0,), (1,)), ((), ())), preferred_element_type=jnp.float32
    )
    vit_grad = out_grad.astype(jnp.float32) + normalize_back(
        normed_grad, in_rows, in_inverse, ln_gain
    )
    return vit_grad.astype(jnp.bfloat16)


bf16, f32 = jnp.bfloat16, jnp.float32


def swap(values, axis, bit):
    count = lax.axis_size(axis)
    return lax.ppermute(values, axis, [(i, i ^ bit) for i in range(count)])


def fits(mesh):
    sections, copies, shards = (mesh.shape[name] for name in ("section", "dp", "vit"))
    return (sections, copies, shards) == (4, 4, 2)


def dot(a, b, ca=1, cb=0):
    return lax.dot_general(a, b, (((ca,), (cb,)), ((), ())), preferred_element_type=f32)


def block_of(size, limit):
    return max(b for b in range(128, limit + 1, 128) if size % b == 0)


def run_kernel(body, grid, in_specs, out_specs, out_shape, scratch=(), prefetch=0, limit=10, cost=0):
    return pl.pallas_call(
        body,
        grid_spec=pltpu.PrefetchScalarGridSpec(
            num_scalar_prefetch=prefetch,
            grid=grid,
            in_specs=in_specs,
            out_specs=out_specs,
            scratch_shapes=list(scratch),
        ),
        out_shape=out_shape,
        cost_estimate=pl.CostEstimate(flops=cost, transcendentals=0, bytes_accessed=0)
        if cost
        else None,
        compiler_params=pltpu.CompilerParams(
            dimension_semantics=("arbitrary",) * len(grid), vmem_limit_bytes=limit << 20
        ),
    )


def whole(array):
    return pl.BlockSpec(array.shape, lambda i, *_: (0,) * array.ndim)


RESIDENT = pl.BlockSpec(memory_space=pltpu.VMEM)


def struct(shape, dtype):
    return jax.ShapeDtypeStruct(shape, dtype)


LANES = 128
COST = 8_000_000_000


def put_rows(ref, first, values):
    for c in range(ref.shape[0]):
        ref[c, first : first + values.shape[0], :] = values[:, c * LANES : (c + 1) * LANES]


def every_fourth(ref, j, count):
    return jnp.concatenate(
        [ref[c, pl.ds(j, count, stride=4), :] for c in range(ref.shape[0])], axis=1
    )


def image_ends(image_ref, images):
    group, ends = lax.axis_index("section"), []
    for k in range(images):
        ends.append(image_ref[k, group] + (ends[-1] if ends else 0))
    return ends


def weighted_sum(section_layer, grad_llm, arrived):
    rows, width = arrived[0].shape

    def body(layer_ref, grad_ref, *refs):
        arrived_refs, (out_ref, own, sem) = refs[:-3], refs[-3:]
        here = lax.axis_index("section")
        window = pl.ds(pl.multiple_of(here * rows, 16), rows)
        copy = pltpu.make_async_copy(grad_ref.at[0, window, :], own, sem)
        copy.start()

        def term(section, values):
            layer = layer_ref[section]
            weight = jnp.where(layer < LEVELS, (layer + 1).astype(f32) / LEVELS, 0.0)
            return weight * values.astype(f32)

        total = sum(term(here ^ (k + 1), ref[...]) for k, ref in enumerate(arrived_refs))
        copy.wait()
        out_ref[...] = (total + term(here, own[...])).astype(bf16)

    return run_kernel(
        body,
        (1,),
        [pl.BlockSpec(memory_space=pl.ANY)] + [whole(x) for x in arrived],
        pl.BlockSpec((rows, width), lambda i, *_: (0, 0)),
        struct((rows, width), bf16),
        [pltpu.VMEM((rows, width), bf16), pltpu.SemaphoreType.DMA],
        prefetch=1,
        limit=4,
    )(section_layer, grad_llm, *arrived)


def own_columns(qkv_weight, proj_weight, shards, copies):
    part_rows, width = proj_weight.shape
    group = qkv_weight.shape[1] // (3 * shards * copies)

    def body(qkv_ref, proj_ref, piece_ref, *part_refs):
        place = lax.axis_index("vit") * copies + lax.axis_index("dp")
        for v in range(shards):
            for q in range(copies):

                @pl.when(place == v * copies + q)
                def _(v=v, q=q):
                    for p in range(copies):
                        first = (v * copies + (q ^ p)) * group
                        cols = jnp.concatenate(
                            [qkv_ref[:, c * width + first : c * width + first + group] for c in range(3)],
                            axis=1,
                        )
                        part_refs[p][...] = cols
                        if p == 0:
                            columns = proj_ref[:, q * part_rows : (q + 1) * part_rows]
                            piece_ref[...] = jnp.concatenate([cols, columns], axis=1)

    shapes = [(part_rows, 3 * group + part_rows)] + [(part_rows, 3 * group)] * copies
    return run_kernel(
        body,
        (1,),
        [whole(qkv_weight), whole(proj_weight)],
        [pl.BlockSpec(shape, lambda i, *_: (0, 0)) for shape in shapes],
        [struct(shape, bf16) for shape in shapes],
        limit=16,
        cost=COST,
    )(qkv_weight, proj_weight)


def slope_of(own, other, gain, bias, fc1_weight, fc1_bias):
    patches, width = own.shape
    slots = patches * 2 // 4
    depth, hidden = fc1_weight.shape
    block = block_of(hidden, 256)
    steps = hidden // block

    def body(own_ref, other_ref, gain_ref, bias_ref, fc1b_ref, fc1_ref, out_ref, x, m):
        put_rows(x, 0, own_ref[...].astype(f32))
        put_rows(x, patches, other_ref[...].astype(f32))
        gain, bias = gain_ref[...].reshape(1, width), bias_ref[...].reshape(1, width)
        for j in range(4):
            rows, _ = normalize(every_fourth(x, j, slots))
            m[:, j * width : (j + 1) * width] = (rows * gain + bias).astype(bf16)

        def step(i, carry):
            window = pl.ds(pl.multiple_of(i * block, LANES), block)
            pre_act = dot(m[...], fc1_ref[:, window]) + fc1b_ref[window].reshape(1, block)
            out_ref[:, window] = gelu_slope(pre_act)
            return carry

        lax.fori_loop(0, steps, step, 0)

    return run_kernel(
        body,
        (1,),
        [whole(x) for x in (own, other, gain, bias, fc1_bias)]
        + [RESIDENT],
        pl.BlockSpec((slots, hidden), lambda i, *_: (0, 0)),
        struct((slots, hidden), f32),
        [
            pltpu.VMEM((width // LANES, 2 * patches, LANES), f32),
            pltpu.VMEM((slots, depth), bf16),
        ],
        cost=COST,
        limit=5,
    )(own, other, gain, bias, fc1_bias, fc1_weight)


def pre_grad_of(image_rows, vis_slot, own, other, fc2_weight, slope):
    rows, width = own.shape
    slots, hidden = slope.shape
    half = slots // 2
    llm_rows = vis_slot.shape[1]
    images = image_rows.shape[0]
    block = block_of(hidden, 256)
    steps = hidden // block

    def body(
        image_ref, slot_ref, own_ref, other_ref, slope_ref, fc2_ref, out_ref, merged, buffer, sems
    ):
        def fetch(i):
            rows_here = pl.ds(pl.multiple_of(i * block, LANES), block)
            return pltpu.make_async_copy(fc2_ref.at[rows_here, :], buffer.at[i], sems.at[i])

        for i in range(steps):
            fetch(i).start()
        section, shard = lax.axis_index("section"), lax.axis_index("vit")
        index = lax.broadcasted_iota(jnp.int32, (slots, llm_rows), 0)
        position = ((index // half) ^ shard) * half + index % half
        live = position < image_ends(image_ref, images)[-1]
        shift = (
            lax.broadcasted_iota(jnp.int32, (llm_rows, rows), 0)
            == lax.broadcasted_iota(jnp.int32, (llm_rows, rows), 1) + section * rows
        ).astype(bf16)
        chosen = []
        for part in range(2):
            named = slot_ref[pl.ds(shard ^ part, 1), :] - section * slots
            found = ((position == named) & live).astype(f32).astype(bf16)
            chosen.append(dot(found, shift))
        chosen = jnp.concatenate(chosen, axis=1).astype(bf16)
        total = dot(chosen, jnp.concatenate([own_ref[...], other_ref[...]], axis=0))
        merged[...] = total.astype(bf16)

        def step(i, carry):
            window = pl.ds(pl.multiple_of(i * block, LANES), block)
            fetch(i).wait()
            hidden_grad = dot(merged[...], buffer[i], 1, 1)
            out_ref[:, window] = (hidden_grad * slope_ref[:, window]).astype(bf16)
            return carry

        lax.fori_loop(0, steps, step, 0)

    return run_kernel(
        body,
        (1,),
        [whole(x) for x in (vis_slot, own, other, slope)] + [pl.BlockSpec(memory_space=pltpu.HBM)],
        pl.BlockSpec((slots, hidden), lambda i, *_: (0, 0)),
        struct((slots, hidden), bf16),
        [
            pltpu.VMEM((slots, width), bf16),
            pltpu.VMEM((steps, block, width), bf16),
            pltpu.SemaphoreType.DMA((steps,)),
        ],
        prefetch=1,
        limit=22,
    )(
        image_rows,
        vis_slot,
        own,
        other,
        slope,
        pltpu.with_memory_space_constraint(fc2_weight, pltpu.HBM),
    )


def merge_part(pre_grad, fc1_weight, part, parts):
    slots, _ = pre_grad.shape
    columns = fc1_weight.shape[0] // parts
    block = block_of(columns, 256)
    steps = columns // block

    def body(pre_ref, fc1_ref, out_ref):
        def step(i, carry):
            window = pl.ds(pl.multiple_of(i * block, LANES), block)
            rows = pl.ds(pl.multiple_of(part * columns + i * block, LANES), block)
            out_ref[:, window] = dot(pre_ref[...], fc1_ref[rows, :], 1, 1).astype(bf16)
            return carry

        lax.fori_loop(0, steps, step, 0)

    return run_kernel(
        body,
        (1,),
        [whole(pre_grad), RESIDENT],
        pl.BlockSpec((slots, columns), lambda i, *_: (0, 0)),
        struct((slots, columns), bf16),
        limit=2,
    )(pre_grad, fc1_weight)


def project(own, other, gain, bias, weights, head_dim):
    patches, width = own.shape
    length = 2 * patches
    slots = length // 4
    sections, copies = len(weights), len(weights[0])
    part_rows, group_cols = weights[0][0].shape
    pieces = group_cols // head_dim
    flat = [w for parts in weights for w in parts]

    def body(own_ref, other_ref, gain_ref, bias_ref, *refs):
        w_refs, (out_ref, x, n) = refs[: len(flat)], refs[len(flat) :]
        section = lax.axis_index("section")
        put_rows(x, 0, own_ref[...].astype(f32))
        put_rows(x, patches, other_ref[...].astype(f32))
        gain, bias = gain_ref[...].reshape(1, width), bias_ref[...].reshape(1, width)
        for j in range(4):
            rows, _ = normalize(every_fourth(x, j, slots))
            rows = (rows * gain + bias).astype(bf16)
            for t in range(sections):
                n[t, j * slots : (j + 1) * slots, :] = rows[:, t * part_rows : (t + 1) * part_rows]
        for p in range(copies):
            total = sum(
                dot(n[section ^ k], w_refs[k * copies + p][:, :group_cols])
                for k in range(sections)
            ).T
            for c in range(pieces):
                out_ref[p, c] = total[c * head_dim : (c + 1) * head_dim].astype(bf16)

    shape = (copies, pieces, head_dim, length)
    return run_kernel(
        body,
        (1,),
        [whole(x) for x in (own, other, gain, bias, *flat)],
        pl.BlockSpec(shape, lambda i, *_: (0, 0, 0, 0)),
        struct(shape, bf16),
        [
            pltpu.VMEM((width // LANES, length, LANES), f32),
            pltpu.VMEM((sections, length, part_rows), bf16),
        ],
        limit=30,
    )(own, other, gain, bias, *flat)


def attention_back(
    image_rows, own, other, gain, mine, theirs, proj_weight, proj_apart, projected, weights, head_dim
):
    patches, width = own.shape
    length = 2 * patches
    slots = length // 4
    half = slots // 2
    images = image_rows.shape[0]
    sections, copies = len(weights), len(weights[0])
    part_rows, group_cols = weights[0][0].shape
    group_heads = group_cols // (3 * head_dim)
    part_heads = part_rows // head_dim
    shard_sections = copies * group_heads // part_heads
    flat = [w for parts in weights for w in parts]
    apart = list(proj_apart)
    chunks = len(mine)
    per_chunk = 4 // chunks
    score_scale = head_dim ** (-0.5)

    def body(image_ref, own_ref, other_ref, gain_ref, *refs):
        gain = gain_ref[...].reshape(1, width)
        mine_refs, refs = refs[:chunks], refs[chunks:]
        theirs_refs, refs = refs[:chunks], refs[chunks:]
        proj_ref, projected_ref, refs = refs[0], refs[1], refs[2:]
        w_refs, refs = refs[: len(flat)], refs[len(flat) :]
        apart_refs, refs = dict(zip(apart, refs)), refs[len(apart) :]
        own_out, other_out, grad_out, x, og, og_parts, heads, acc = refs
        section, shard, copy = (lax.axis_index(name) for name in ("section", "vit", "dp"))
        ends = image_ends(image_ref, images)
        put_rows(x, 0, own_ref[...].astype(f32))
        put_rows(x, patches, other_ref[...].astype(f32))
        for j in range(4):
            rows, inverse = normalize(every_fourth(x, j, slots))
            cols = slice(j % per_chunk * width, (j % per_chunk + 1) * width)
            there = theirs_refs[j // per_chunk][:, cols]
            there = jnp.concatenate([there[half:], there[:half]], axis=0)
            upstream = mine_refs[j // per_chunk][:, cols].astype(f32) + there.astype(f32)
            result = normalize_back(upstream, rows, inverse, gain).astype(bf16)
            og[j * slots : (j + 1) * slots, :] = result
            grad_out[j] = result[:half]
            for t in range(sections):
                og_parts[t, j * slots : (j + 1) * slots, :] = result[
                    :, t * part_rows : (t + 1) * part_rows
                ]

        def put_heads(part, cols):
            for h in range(part_heads):
                heads[part * part_heads + h] = cols[h * head_dim : (h + 1) * head_dim].astype(bf16)

        for i in range(shard_sections):
            relation = section ^ (shard * shard_sections + i)
            for k in range(sections):

                @pl.when(relation == k)
                def _(i=i, k=k):
                    if k == 0:
                        put_heads(i, dot(proj_ref[...], og[...], 1, 1))
                    else:
                        fetched = [
                            apart_refs[k, p][...]
                            if (k, p) in apart_refs
                            else w_refs[k * copies + p][:, group_cols : group_cols + part_rows]
                            for p in range(copies)
                        ]
                        put_heads(
                            i, sum(dot(w, og_parts[copy ^ p], 1, 1) for p, w in enumerate(fetched))
                        )

        def image_of(axis):
            index = lax.broadcasted_iota(jnp.int32, (length, length), axis) % slots
            position = ((index // half) ^ shard) * half + index % half
            image = jnp.zeros((length, length), jnp.int32)
            for e in range(images):
                image += (position >= ends[e]).astype(jnp.int32)
            return image

        image = image_of(0)
        allowed = (image == image_of(1)) & (image < images)
        dead = (image_of(1)[:1] == images).astype(f32)
        for p in range(copies):
            grads = [[], [], []]
            for h in range(group_heads):
                query, key, value = (projected_ref[p, c * group_heads + h] for c in range(3))
                grad = heads[(copy ^ p) * group_heads + h]
                scores = dot(key, query, 0, 0) * score_scale
                exponent = jnp.where(allowed, jnp.exp(scores), 0.0)
                denominator = jnp.sum(exponent, axis=0, keepdims=True) + dead
                softmax_weights = (exponent / denominator).astype(bf16)
                prob_grad = dot(value, grad, 0, 0)
                weighted = softmax_weights.astype(f32)
                row_dot = jnp.sum(weighted * prob_grad, axis=0, keepdims=True)
                score_grad = (weighted * (prob_grad - row_dot) * score_scale).astype(bf16)
                grads[0].append(dot(key, score_grad))
                grads[1].append(dot(query, score_grad, 1, 1))
                grads[2].append(dot(grad, softmax_weights, 1, 1))
            group_grad = jnp.concatenate([g for gs in grads for g in gs], axis=0).astype(bf16)
            for k in range(sections):
                term = dot(w_refs[k * copies + p][:, :group_cols], group_grad)
                acc[k] = term if p == 0 else acc[k] + term

        result = jnp.concatenate([acc[section ^ t] for t in range(sections)], axis=0).T
        for j in range(4):
            own_out[j] = result[j * slots : j * slots + half]
            other_out[j] = result[j * slots + half : (j + 1) * slots].astype(bf16)

    shape = (4, half, width)
    operands = (own, other, gain, *mine, *theirs, proj_weight, projected, *flat, *proj_apart.values())
    return run_kernel(
        body,
        (1,),
        [whole(x) for x in operands],
        [pl.BlockSpec(shape, lambda i, *_: (0, 0, 0))] * 3,
        [struct(shape, f32), struct(shape, bf16), struct(shape, bf16)],
        [
            pltpu.VMEM((width // LANES, length, LANES), f32),
            pltpu.VMEM((length, width), bf16),
            pltpu.VMEM((sections, length, part_rows), bf16),
            pltpu.VMEM((copies * group_heads, head_dim, length), bf16),
            pltpu.VMEM((sections, part_rows, length), f32),
        ],
        prefetch=1,
        limit=40,
    )(image_rows, *operands)


def finish(own, gain, mine, theirs, out_grad):
    patches, width = own.shape

    def body(own_ref, gain_ref, mine_ref, theirs_ref, grad_ref, out_ref, x):
        gain = gain_ref[...].reshape(1, width)
        put_rows(x, 0, own_ref[...].astype(f32))
        for j in range(4):
            rows, inverse = normalize(every_fourth(x, j, patches // 4))
            upstream = mine_ref[j] + theirs_ref[j].astype(f32)
            result = grad_ref[j].astype(f32) + normalize_back(
                upstream, rows, inverse, gain
            )
            for c in range(x.shape[0]):
                x[c, pl.ds(j, patches // 4, stride=4), :] = result[:, c * LANES : (c + 1) * LANES]
        out_ref[...] = jnp.concatenate([x[c] for c in range(x.shape[0])], axis=1).astype(bf16)

    operands = (own, gain, mine, theirs, out_grad)
    return run_kernel(
        body,
        (1,),
        [whole(x) for x in operands],
        pl.BlockSpec((patches, width), lambda i, *_: (0, 0)),
        struct((patches, width), bf16),
        [pltpu.VMEM((width // LANES, patches, LANES), f32)],
    )(*operands)


def local_paired(
    grad_llm,
    vis_slot,
    image_rows,
    section_layer,
    vit_in,
    vit_out,
    ln_gain,
    ln_bias,
    qkv_weight,
    proj_weight,
    merge_gain,
    merge_bias,
    fc1_weight,
    fc1_bias,
    fc2_weight,
):
    sections = lax.axis_size("section")
    shards = lax.axis_size("vit")
    copies = lax.axis_size("dp")
    section_index = lax.axis_index("section")
    llm_width = grad_llm.shape[2]
    vit_width = vit_in.shape[1]
    head_dim = vit_width // HEADS
    group_rows = grad_llm.shape[1] // sections
    image_rows = image_rows.T

    outgoing = grad_llm[0].reshape(sections, group_rows, llm_width)
    arrived = {
        k: swap(
            lax.dynamic_index_in_dim(outgoing, section_index ^ k, 0, keepdims=False), "section", k
        )
        for k in range(1, sections)
    }
    vit_out_other = swap(vit_out, "vit", 1)
    piece, *own_parts = own_columns(qkv_weight, proj_weight, shards, copies)
    near = swap(piece, "section", 1)
    far = swap(piece, "section", 2)
    vit_in_other = swap(vit_in, "vit", 1)
    slope = slope_of(vit_out, vit_out_other, merge_gain, merge_bias, fc1_weight, fc1_bias)
    arrived, slope = lax.optimization_barrier((arrived, slope))

    summed = weighted_sum(section_layer, grad_llm, [arrived[k] for k in range(1, sections)])
    summed_other = swap(summed, "vit", 1)
    near, summed_other = lax.optimization_barrier((near, summed_other))
    near_chip = swap(near, "dp", 2)
    near_core = swap(near, "dp", 1)

    pre_grad = pre_grad_of(image_rows, vis_slot, summed, summed_other, fc2_weight, slope)
    far, near_chip, pre_grad = lax.optimization_barrier((far, near_chip, pre_grad))
    cross = swap(far, "section", 1)
    far_chip = swap(far, "dp", 2)
    near_diagonal = swap(near_chip, "dp", 1)
    far_core = swap(far, "dp", 1)
    first = merge_part(pre_grad, fc1_weight, 0, 2)
    first_theirs = swap(first, "vit", 1)
    second = merge_part(pre_grad, fc1_weight, 1, 2)
    second, cross, far_chip = lax.optimization_barrier((second, cross, far_chip))
    columns = own_parts[1].shape[1]
    cross_chip = swap(cross[:, :columns], "dp", 2)
    late_proj = swap(far_chip[:, columns:], "section", 1)
    second_theirs = swap(second, "vit", 1)
    cross_core = swap(cross, "dp", 1)
    far_diagonal = swap(far_chip, "dp", 1)
    cross_chip, late_proj = lax.optimization_barrier((cross_chip, late_proj))
    cross_diagonal = swap(cross_chip, "dp", 1)
    late_proj_core = swap(late_proj, "dp", 1)
    weights = [
        own_parts,
        [near, near_core, near_chip, near_diagonal],
        [far, far_core, far_chip, far_diagonal],
        [cross, cross_core, cross_chip, cross_diagonal],
    ]
    proj_apart = {(3, 2): late_proj, (3, 3): late_proj_core}

    projected = project(vit_in, vit_in_other, ln_gain, ln_bias, weights, head_dim)
    normed_mine, normed_sent, out_grad = attention_back(
        image_rows,
        vit_out,
        vit_out_other,
        merge_gain,
        [first, second],
        [first_theirs, second_theirs],
        proj_weight,
        proj_apart,
        projected,
        weights,
        head_dim,
    )
    normed_theirs = swap(normed_sent, "vit", 1)
    return finish(vit_in, ln_gain, normed_mine, normed_theirs, out_grad)


def solution(mesh):
    paired = fits(mesh)

    def chosen_form(*arguments):
        return (local_paired if paired else local)(*arguments)

    placed = (
        P("section", ("dp", "vit"), None),
        P("dp", None),
        P("dp", None),
        P(),
        P(("dp", "section", "vit"), None),
        P(("dp", "section", "vit"), None),
        P(),
        P(),
        P("section", None),
        P("section", None),
        P(),
        P(),
        P(None, "vit"),
        P("vit"),
        P("vit", None),
    )
    return jax.shard_map(
        chosen_form,
        mesh=mesh,
        in_specs=placed,
        out_specs=P(("dp", "section", "vit"), None),
        check_vma=False,
    )
```

```python
import jax
import jax.numpy as jnp
from jax import lax
from jax.experimental import pallas as pl
from jax.experimental.pallas import tpu as pltpu
from jax.sharding import PartitionSpec as P

HEADS = 16
LEVELS = 3


norm_eps = 1e-06


def normalize(values):
    row_mean = jnp.mean(values, axis=-1, keepdims=True)
    centered = values - row_mean
    variance = jnp.mean(centered * centered, axis=-1, keepdims=True)
    inverse = lax.rsqrt(variance + norm_eps)
    return (centered * inverse, inverse)


def normalize_back(upstream, normed_rows, inverse, gain):
    scaled = upstream * gain
    mean_scaled = jnp.mean(scaled, axis=-1, keepdims=True)
    mean_cross = jnp.mean(scaled * normed_rows, axis=-1, keepdims=True)
    return (scaled - mean_scaled - normed_rows * mean_cross) * inverse


def gelu_slope(pre_act):
    cumulative = 0.5 * (1.0 + lax.erf(pre_act * 0.7071067811865476))
    density = jnp.exp(-0.5 * pre_act * pre_act) * 0.3989422804014327
    return cumulative + pre_act * density


def local(
    grad_llm,
    vis_slot,
    image_rows,
    section_layer,
    vit_in,
    vit_out,
    ln_gain,
    ln_bias,
    qkv_weight,
    proj_weight,
    merge_gain,
    merge_bias,
    fc1_weight,
    fc1_bias,
    fc2_weight,
):
    sections = lax.axis_size("section")
    shards = lax.axis_size("vit")
    section_index = lax.axis_index("section")
    shard_index = lax.axis_index("vit")
    devices = sections * shards
    patches = vit_in.shape[0]
    slots_here = patches // 4
    run_rows = grad_llm.shape[1] // devices
    llm_width = grad_llm.shape[2]
    vit_width = vit_in.shape[1]
    head_dim = vit_width // HEADS
    device_index = section_index * shards + shard_index
    qkv_full, proj_full = (
        lax.all_gather(qkv_weight, "section", axis=0, tiled=True),
        lax.all_gather(proj_weight, "section", axis=0, tiled=True),
    )
    in_rows, in_inverse = normalize(vit_in.astype(jnp.float32))
    normed = (in_rows * ln_gain + ln_bias).astype(jnp.bfloat16)
    projected = lax.dot_general(
        qkv_full, normed, (((0,), (1,)), ((), ())), preferred_element_type=jnp.float32
    )
    projected = projected.astype(jnp.bfloat16).reshape(3, HEADS, head_dim, patches)
    section_weight = jnp.where(
        section_layer < LEVELS, (section_layer + 1).astype(jnp.float32) / LEVELS, 0.0
    )
    outgoing = grad_llm[0].reshape(devices, run_rows, llm_width)
    image_ends = jnp.cumsum(image_rows[section_index])
    out_rows, out_inverse = normalize(vit_out.astype(jnp.float32))
    merge_in = (
        (out_rows * merge_gain + merge_bias).astype(jnp.bfloat16).reshape(slots_here, 4 * vit_width)
    )
    arrived = lax.all_to_all(outgoing, ("section", "vit"), split_axis=0, concat_axis=0, tiled=True)
    arrived_f = arrived.reshape(sections, shards, run_rows, llm_width).astype(jnp.float32)
    incoming = jnp.sum(arrived_f * section_weight[:, None, None, None], axis=0)
    columns = lax.dynamic_slice_in_dim(vis_slot, device_index * run_rows, run_rows, 1)
    local_slot = (columns - device_index * slots_here).reshape(-1)
    placed = (
        jnp.zeros((slots_here, llm_width), jnp.float32)
        .at[local_slot]
        .set(incoming.reshape(-1, llm_width))
    )
    slot_position = shard_index * slots_here + jnp.arange(slots_here, dtype=jnp.int32)
    merged_grad = jnp.where((slot_position < image_ends[-1])[:, None], placed, 0.0).astype(
        jnp.bfloat16
    )
    rows_in, rows_grad = (
        lax.all_gather(merge_in, "vit", axis=0, tiled=True),
        lax.all_gather(merged_grad, "vit", axis=0, tiled=True),
    )
    pre_act = jnp.dot(rows_in, fc1_weight, preferred_element_type=jnp.float32) + fc1_bias
    hidden_grad = lax.dot_general(
        rows_grad, fc2_weight, (((1,), (1,)), ((), ())), preferred_element_type=jnp.float32
    )
    pre_grad = (hidden_grad * gelu_slope(pre_act)).astype(jnp.bfloat16)
    merge_grad = lax.psum_scatter(
        lax.dot_general(
            pre_grad, fc1_weight, (((1,), (1,)), ((), ())), preferred_element_type=jnp.float32
        ).astype(jnp.bfloat16),
        "vit",
        scatter_dimension=0,
        tiled=True,
    ).astype(jnp.float32)
    out_grad = normalize_back(
        merge_grad.reshape(patches, vit_width), out_rows, out_inverse, merge_gain
    ).astype(jnp.bfloat16)
    grad_cols = lax.dot_general(
        proj_full, out_grad, (((1,), (1,)), ((), ())), preferred_element_type=jnp.float32
    )
    grad_cols = grad_cols.astype(jnp.bfloat16).reshape(1, HEADS, head_dim, patches)
    head_inputs, head_grad = (
        lax.all_to_all(projected, "vit", split_axis=1, concat_axis=3, tiled=True),
        lax.all_to_all(grad_cols, "vit", split_axis=1, concat_axis=3, tiled=True),
    )
    length = shards * patches
    block_size = min(512, length)
    block_count = length // block_size
    slot_of = jnp.arange(length, dtype=jnp.int32) // 4
    patch_image = jnp.sum((slot_of[:, None] >= image_ends[None, :]).astype(jnp.int32), axis=1)
    patch_live = slot_of < image_ends[-1]
    score_scale = head_dim ** (-0.5)
    contract_first = (((0,), (0,)), ((), ()))

    def head_backward(query_cols, key_cols, value_cols, grad_head):

        def step(carry, block_index):
            key_acc, value_acc = carry
            first_row = block_index * block_size
            query_block = lax.dynamic_slice_in_dim(query_cols, first_row, block_size, 1)
            grad_block = lax.dynamic_slice_in_dim(grad_head, first_row, block_size, 1)
            image_block = lax.dynamic_slice_in_dim(patch_image, first_row, block_size, 0)
            live_block = lax.dynamic_slice_in_dim(patch_live, first_row, block_size, 0)
            scores = (
                lax.dot_general(
                    query_block, key_cols, contract_first, preferred_element_type=jnp.float32
                )
                * score_scale
            )
            allowed = (
                (image_block[:, None] == patch_image[None, :])
                & live_block[:, None]
                & patch_live[None, :]
            )
            exponent = jnp.where(allowed, jnp.exp(jnp.where(allowed, scores, 0.0)), 0.0)
            denominator = (
                jnp.sum(exponent, axis=1, keepdims=True)
                + 1.0
                - live_block.astype(jnp.float32)[:, None]
            )
            softmax_weights = (exponent / denominator).astype(jnp.bfloat16)
            prob_grad = lax.dot_general(
                grad_block, value_cols, contract_first, preferred_element_type=jnp.float32
            )
            weighted = softmax_weights.astype(jnp.float32)
            row_dot = jnp.sum(weighted * prob_grad, axis=1, keepdims=True)
            score_grad = (weighted * (prob_grad - row_dot) * score_scale).astype(jnp.bfloat16)
            query_grad = lax.dot_general(
                key_cols, score_grad, (((1,), (1,)), ((), ())), preferred_element_type=jnp.float32
            )
            key_acc = key_acc + lax.dot_general(
                query_block,
                score_grad,
                (((1,), (0,)), ((), ())),
                preferred_element_type=jnp.float32,
            )
            value_acc = value_acc + lax.dot_general(
                grad_block,
                softmax_weights,
                (((1,), (0,)), ((), ())),
                preferred_element_type=jnp.float32,
            )
            return ((key_acc, value_acc), query_grad.astype(jnp.bfloat16))

        empty = jnp.zeros((head_dim, length), jnp.float32)
        (key_total, value_total), query_blocks = lax.scan(
            step, (empty, empty), jnp.arange(block_count, dtype=jnp.int32)
        )
        query_total = query_blocks.transpose(1, 0, 2).reshape(head_dim, length)
        return (query_total, key_total.astype(jnp.bfloat16), value_total.astype(jnp.bfloat16))

    query_all, key_all, value_all = jax.vmap(head_backward)(
        head_inputs[0], head_inputs[1], head_inputs[2], head_grad[0]
    )
    head_result = jnp.stack([query_all, key_all, value_all])
    returned = lax.all_to_all(head_result, "vit", split_axis=3, concat_axis=1, tiled=True)
    projected_grad = returned.reshape(3 * vit_width, patches)
    normed_grad = lax.dot_general(
        projected_grad, qkv_full, (((0,), (1,)), ((), ())), preferred_element_type=jnp.float32
    )
    vit_grad = out_grad.astype(jnp.float32) + normalize_back(
        normed_grad, in_rows, in_inverse, ln_gain
    )
    return vit_grad.astype(jnp.bfloat16)


bf16, f32 = jnp.bfloat16, jnp.float32


def swap(values, axis, bit):
    count = lax.axis_size(axis)
    return lax.ppermute(values, axis, [(i, i ^ bit) for i in range(count)])


def fits(mesh):
    sections, copies, shards = (mesh.shape[name] for name in ("section", "dp", "vit"))
    return (sections, copies, shards) == (4, 4, 2)


def dot(a, b, ca=1, cb=0):
    return lax.dot_general(a, b, (((ca,), (cb,)), ((), ())), preferred_element_type=f32)


def block_of(size, limit):
    return max(b for b in range(128, limit + 1, 128) if size % b == 0)


def run_kernel(body, grid, in_specs, out_specs, out_shape, scratch=(), prefetch=0, limit=10, cost=0):
    return pl.pallas_call(
        body,
        grid_spec=pltpu.PrefetchScalarGridSpec(
            num_scalar_prefetch=prefetch,
            grid=grid,
            in_specs=in_specs,
            out_specs=out_specs,
            scratch_shapes=list(scratch),
        ),
        out_shape=out_shape,
        cost_estimate=pl.CostEstimate(flops=cost, transcendentals=0, bytes_accessed=0)
        if cost
        else None,
        compiler_params=pltpu.CompilerParams(
            dimension_semantics=("arbitrary",) * len(grid), vmem_limit_bytes=limit << 20
        ),
    )


def whole(array):
    return pl.BlockSpec(array.shape, lambda i, *_: (0,) * array.ndim)


RESIDENT = pl.BlockSpec(memory_space=pltpu.VMEM)


def struct(shape, dtype):
    return jax.ShapeDtypeStruct(shape, dtype)


LANES = 128
COST = 8_000_000_000


def put_rows(ref, first, values):
    for c in range(ref.shape[0]):
        ref[c, first : first + values.shape[0], :] = values[:, c * LANES : (c + 1) * LANES]


def every_fourth(ref, j, count):
    return jnp.concatenate(
        [ref[c, pl.ds(j, count, stride=4), :] for c in range(ref.shape[0])], axis=1
    )


def image_ends(image_ref, images):
    group, ends = lax.axis_index("section"), []
    for k in range(images):
        ends.append(image_ref[k, group] + (ends[-1] if ends else 0))
    return ends


def weighted_sum(section_layer, grad_llm, arrived):
    rows, width = arrived[0].shape

    def body(layer_ref, grad_ref, *refs):
        arrived_refs, (out_ref, own, sem) = refs[:-3], refs[-3:]
        here = lax.axis_index("section")
        window = pl.ds(pl.multiple_of(here * rows, 16), rows)
        copy = pltpu.make_async_copy(grad_ref.at[0, window, :], own, sem)
        copy.start()

        def term(section, values):
            layer = layer_ref[section]
            weight = jnp.where(layer < LEVELS, (layer + 1).astype(f32) / LEVELS, 0.0)
            return weight * values.astype(f32)

        total = sum(term(here ^ (k + 1), ref[...]) for k, ref in enumerate(arrived_refs))
        copy.wait()
        out_ref[...] = (total + term(here, own[...])).astype(bf16)

    return run_kernel(
        body,
        (1,),
        [pl.BlockSpec(memory_space=pl.ANY)] + [whole(x) for x in arrived],
        pl.BlockSpec((rows, width), lambda i, *_: (0, 0)),
        struct((rows, width), bf16),
        [pltpu.VMEM((rows, width), bf16), pltpu.SemaphoreType.DMA],
        prefetch=1,
        limit=4,
    )(section_layer, grad_llm, *arrived)


def own_columns(qkv_weight, proj_weight, shards, copies):
    part_rows, width = proj_weight.shape
    group = qkv_weight.shape[1] // (3 * shards * copies)

    def body(qkv_ref, proj_ref, piece_ref, *part_refs):
        place = lax.axis_index("vit") * copies + lax.axis_index("dp")
        for v in range(shards):
            for q in range(copies):

                @pl.when(place == v * copies + q)
                def _(v=v, q=q):
                    for p in range(copies):
                        first = (v * copies + (q ^ p)) * group
                        cols = jnp.concatenate(
                            [qkv_ref[:, c * width + first : c * width + first + group] for c in range(3)],
                            axis=1,
                        )
                        part_refs[p][...] = cols
                        if p == 0:
                            columns = proj_ref[:, q * part_rows : (q + 1) * part_rows]
                            piece_ref[...] = jnp.concatenate([cols, columns], axis=1)

    shapes = [(part_rows, 3 * group + part_rows)] + [(part_rows, 3 * group)] * copies
    return run_kernel(
        body,
        (1,),
        [whole(qkv_weight), whole(proj_weight)],
        [pl.BlockSpec(shape, lambda i, *_: (0, 0)) for shape in shapes],
        [struct(shape, bf16) for shape in shapes],
        limit=16,
        cost=COST,
    )(qkv_weight, proj_weight)


def slope_of(own, other, gain, bias, fc1_weight, fc1_bias):
    patches, width = own.shape
    slots = patches * 2 // 4
    depth, hidden = fc1_weight.shape
    block = block_of(hidden, 256)
    steps = hidden // block

    def body(own_ref, other_ref, gain_ref, bias_ref, fc1b_ref, fc1_ref, out_ref, x, m):
        put_rows(x, 0, own_ref[...].astype(f32))
        put_rows(x, patches, other_ref[...].astype(f32))
        gain, bias = gain_ref[...].reshape(1, width), bias_ref[...].reshape(1, width)
        for j in range(4):
            rows, _ = normalize(every_fourth(x, j, slots))
            m[:, j * width : (j + 1) * width] = (rows * gain + bias).astype(bf16)

        def step(i, carry):
            window = pl.ds(pl.multiple_of(i * block, LANES), block)
            pre_act = dot(m[...], fc1_ref[:, window]) + fc1b_ref[window].reshape(1, block)
            out_ref[:, window] = gelu_slope(pre_act)
            return carry

        lax.fori_loop(0, steps, step, 0)

    return run_kernel(
        body,
        (1,),
        [whole(x) for x in (own, other, gain, bias, fc1_bias)]
        + [RESIDENT],
        pl.BlockSpec((slots, hidden), lambda i, *_: (0, 0)),
        struct((slots, hidden), f32),
        [
            pltpu.VMEM((width // LANES, 2 * patches, LANES), f32),
            pltpu.VMEM((slots, depth), bf16),
        ],
        cost=COST,
        limit=5,
    )(own, other, gain, bias, fc1_bias, fc1_weight)


def pre_grad_of(image_rows, vis_slot, own, other, fc2_weight, slope):
    rows, width = own.shape
    slots, hidden = slope.shape
    half = slots // 2
    llm_rows = vis_slot.shape[1]
    images = image_rows.shape[0]
    block = block_of(hidden, 256)
    steps = hidden // block

    def body(
        image_ref, slot_ref, own_ref, other_ref, slope_ref, fc2_ref, out_ref, merged, buffer, sems
    ):
        def fetch(i):
            rows_here = pl.ds(pl.multiple_of(i * block, LANES), block)
            return pltpu.make_async_copy(fc2_ref.at[rows_here, :], buffer.at[i], sems.at[i])

        for i in range(steps):
            fetch(i).start()
        section, shard = lax.axis_index("section"), lax.axis_index("vit")
        index = lax.broadcasted_iota(jnp.int32, (slots, llm_rows), 0)
        position = ((index // half) ^ shard) * half + index % half
        live = position < image_ends(image_ref, images)[-1]
        shift = (
            lax.broadcasted_iota(jnp.int32, (llm_rows, rows), 0)
            == lax.broadcasted_iota(jnp.int32, (llm_rows, rows), 1) + section * rows
        ).astype(bf16)
        chosen = []
        for part in range(2):
            named = slot_ref[pl.ds(shard ^ part, 1), :] - section * slots
            found = ((position == named) & live).astype(f32).astype(bf16)
            chosen.append(dot(found, shift))
        chosen = jnp.concatenate(chosen, axis=1).astype(bf16)
        total = dot(chosen, jnp.concatenate([own_ref[...], other_ref[...]], axis=0))
        merged[...] = total.astype(bf16)

        def step(i, carry):
            window = pl.ds(pl.multiple_of(i * block, LANES), block)
            fetch(i).wait()
            hidden_grad = dot(merged[...], buffer[i], 1, 1)
            out_ref[:, window] = (hidden_grad * slope_ref[:, window]).astype(bf16)
            return carry

        lax.fori_loop(0, steps, step, 0)

    return run_kernel(
        body,
        (1,),
        [whole(x) for x in (vis_slot, own, other, slope)] + [pl.BlockSpec(memory_space=pltpu.HBM)],
        pl.BlockSpec((slots, hidden), lambda i, *_: (0, 0)),
        struct((slots, hidden), bf16),
        [
            pltpu.VMEM((slots, width), bf16),
            pltpu.VMEM((steps, block, width), bf16),
            pltpu.SemaphoreType.DMA((steps,)),
        ],
        prefetch=1,
        limit=22,
    )(
        image_rows,
        vis_slot,
        own,
        other,
        slope,
        pltpu.with_memory_space_constraint(fc2_weight, pltpu.HBM),
    )


def merge_part(pre_grad, fc1_weight, part, parts):
    slots, _ = pre_grad.shape
    columns = fc1_weight.shape[0] // parts
    block = block_of(columns, 256)
    steps = columns // block

    def body(pre_ref, fc1_ref, out_ref):
        def step(i, carry):
            window = pl.ds(pl.multiple_of(i * block, LANES), block)
            rows = pl.ds(pl.multiple_of(part * columns + i * block, LANES), block)
            out_ref[:, window] = dot(pre_ref[...], fc1_ref[rows, :], 1, 1).astype(bf16)
            return carry

        lax.fori_loop(0, steps, step, 0)

    return run_kernel(
        body,
        (1,),
        [whole(pre_grad), RESIDENT],
        pl.BlockSpec((slots, columns), lambda i, *_: (0, 0)),
        struct((slots, columns), bf16),
        limit=2,
    )(pre_grad, fc1_weight)


def project_early(own, other, gain, bias, weights, sections):
    patches, width = own.shape
    slots = 2 * patches // 4
    copies = len(weights[0])
    part_rows, group_cols = weights[0][0].shape
    flat = [w for parts in weights for w in parts]

    def body(own_ref, other_ref, gain_ref, bias_ref, *refs):
        w_refs, (sum_ref, last_ref, x, n) = refs[: len(flat)], refs[len(flat) :]
        section = lax.axis_index("section")
        put_rows(x, 0, own_ref[...].astype(f32))
        put_rows(x, patches, other_ref[...].astype(f32))
        gain, bias = gain_ref[...].reshape(1, width), bias_ref[...].reshape(1, width)
        for j in range(4):
            rows, _ = normalize(every_fourth(x, j, slots))
            rows = (rows * gain + bias).astype(bf16)
            for t in range(sections):
                n[t, j * slots : (j + 1) * slots, :] = rows[:, t * part_rows : (t + 1) * part_rows]
        last_ref[...] = n[section ^ (sections - 1)]
        for p in range(copies):
            sum_ref[p] = sum(
                dot(n[section ^ k], w_refs[k * copies + p][:, :group_cols])
                for k in range(len(weights))
            )

    shapes = [(copies, 2 * patches, group_cols), (2 * patches, part_rows)]
    return run_kernel(
        body,
        (1,),
        [whole(x) for x in (own, other, gain, bias, *flat)],
        [
            pl.BlockSpec(shapes[0], lambda i, *_: (0, 0, 0)),
            pl.BlockSpec(shapes[1], lambda i, *_: (0, 0)),
        ],
        [struct(shapes[0], f32), struct(shapes[1], bf16)],
        [
            pltpu.VMEM((width // LANES, 2 * patches, LANES), f32),
            pltpu.VMEM((sections, 2 * patches, part_rows), bf16),
        ],
        limit=30,
    )(own, other, gain, bias, *flat)


def project_late(sums, rows, weights, head_dim):
    copies, length, group_cols = sums.shape
    pieces = group_cols // head_dim

    def body(sum_ref, rows_ref, *refs):
        w_refs, out_ref = refs[:-1], refs[-1]
        for p in range(copies):
            total = (sum_ref[p] + dot(rows_ref[...], w_refs[p][:, :group_cols])).T
            for c in range(pieces):
                out_ref[p, c] = total[c * head_dim : (c + 1) * head_dim].astype(bf16)

    shape = (copies, pieces, head_dim, length)
    return run_kernel(
        body,
        (1,),
        [whole(x) for x in (sums, rows, *weights)],
        pl.BlockSpec(shape, lambda i, *_: (0, 0, 0, 0)),
        struct(shape, bf16),
        limit=20,
    )(sums, rows, *weights)


def attention_back(
    image_rows, own, other, gain, mine, theirs, proj_weight, proj_apart, projected, weights, head_dim
):
    patches, width = own.shape
    length = 2 * patches
    slots = length // 4
    half = slots // 2
    images = image_rows.shape[0]
    sections, copies = len(weights), len(weights[0])
    part_rows, group_cols = weights[0][0].shape
    group_heads = group_cols // (3 * head_dim)
    part_heads = part_rows // head_dim
    shard_sections = copies * group_heads // part_heads
    flat = [w for parts in weights for w in parts]
    apart = list(proj_apart)
    chunks = len(mine)
    per_chunk = 4 // chunks
    score_scale = head_dim ** (-0.5)

    def body(image_ref, own_ref, other_ref, gain_ref, *refs):
        gain = gain_ref[...].reshape(1, width)
        mine_refs, refs = refs[:chunks], refs[chunks:]
        theirs_refs, refs = refs[:chunks], refs[chunks:]
        proj_ref, projected_ref, refs = refs[0], refs[1], refs[2:]
        w_refs, refs = refs[: len(flat)], refs[len(flat) :]
        apart_refs, refs = dict(zip(apart, refs)), refs[len(apart) :]
        own_out, other_out, grad_out, x, og, og_parts, heads, acc = refs
        section, shard, copy = (lax.axis_index(name) for name in ("section", "vit", "dp"))
        ends = image_ends(image_ref, images)
        put_rows(x, 0, own_ref[...].astype(f32))
        put_rows(x, patches, other_ref[...].astype(f32))
        for j in range(4):
            rows, inverse = normalize(every_fourth(x, j, slots))
            cols = slice(j % per_chunk * width, (j % per_chunk + 1) * width)
            there = theirs_refs[j // per_chunk][:, cols]
            there = jnp.concatenate([there[half:], there[:half]], axis=0)
            upstream = mine_refs[j // per_chunk][:, cols].astype(f32) + there.astype(f32)
            result = normalize_back(upstream, rows, inverse, gain).astype(bf16)
            og[j * slots : (j + 1) * slots, :] = result
            grad_out[j] = result[:half]
            for t in range(sections):
                og_parts[t, j * slots : (j + 1) * slots, :] = result[
                    :, t * part_rows : (t + 1) * part_rows
                ]

        def put_heads(part, cols):
            for h in range(part_heads):
                heads[part * part_heads + h] = cols[h * head_dim : (h + 1) * head_dim].astype(bf16)

        for i in range(shard_sections):
            relation = section ^ (shard * shard_sections + i)
            for k in range(sections):

                @pl.when(relation == k)
                def _(i=i, k=k):
                    if k == 0:
                        put_heads(i, dot(proj_ref[...], og[...], 1, 1))
                    else:
                        fetched = [
                            apart_refs[k, p][...]
                            if (k, p) in apart_refs
                            else w_refs[k * copies + p][:, group_cols : group_cols + part_rows]
                            for p in range(copies)
                        ]
                        put_heads(
                            i, sum(dot(w, og_parts[copy ^ p], 1, 1) for p, w in enumerate(fetched))
                        )

        def image_of(axis):
            index = lax.broadcasted_iota(jnp.int32, (length, length), axis) % slots
            position = ((index // half) ^ shard) * half + index % half
            image = jnp.zeros((length, length), jnp.int32)
            for e in range(images):
                image += (position >= ends[e]).astype(jnp.int32)
            return image

        image = image_of(0)
        allowed = (image == image_of(1)) & (image < images)
        dead = (image_of(1)[:1] == images).astype(f32)
        for p in range(copies):
            grads = [[], [], []]
            for h in range(group_heads):
                query, key, value = (projected_ref[p, c * group_heads + h] for c in range(3))
                grad = heads[(copy ^ p) * group_heads + h]
                scores = dot(key, query, 0, 0) * score_scale
                exponent = jnp.where(allowed, jnp.exp(scores), 0.0)
                denominator = jnp.sum(exponent, axis=0, keepdims=True) + dead
                softmax_weights = (exponent / denominator).astype(bf16)
                prob_grad = dot(value, grad, 0, 0)
                weighted = softmax_weights.astype(f32)
                row_dot = jnp.sum(weighted * prob_grad, axis=0, keepdims=True)
                score_grad = (weighted * (prob_grad - row_dot) * score_scale).astype(bf16)
                grads[0].append(dot(key, score_grad))
                grads[1].append(dot(query, score_grad, 1, 1))
                grads[2].append(dot(grad, softmax_weights, 1, 1))
            group_grad = jnp.concatenate([g for gs in grads for g in gs], axis=0).astype(bf16)
            for k in range(sections):
                term = dot(w_refs[k * copies + p][:, :group_cols], group_grad)
                acc[k] = term if p == 0 else acc[k] + term

        result = jnp.concatenate([acc[section ^ t] for t in range(sections)], axis=0).T
        for j in range(4):
            own_out[j] = result[j * slots : j * slots + half]
            other_out[j] = result[j * slots + half : (j + 1) * slots].astype(bf16)

    shape = (4, half, width)
    operands = (own, other, gain, *mine, *theirs, proj_weight, projected, *flat, *proj_apart.values())
    return run_kernel(
        body,
        (1,),
        [whole(x) for x in operands],
        [pl.BlockSpec(shape, lambda i, *_: (0, 0, 0))] * 3,
        [struct(shape, f32), struct(shape, bf16), struct(shape, bf16)],
        [
            pltpu.VMEM((width // LANES, length, LANES), f32),
            pltpu.VMEM((length, width), bf16),
            pltpu.VMEM((sections, length, part_rows), bf16),
            pltpu.VMEM((copies * group_heads, head_dim, length), bf16),
            pltpu.VMEM((sections, part_rows, length), f32),
        ],
        prefetch=1,
        limit=40,
    )(image_rows, *operands)


def finish(own, gain, mine, theirs, out_grad):
    patches, width = own.shape

    def body(own_ref, gain_ref, mine_ref, theirs_ref, grad_ref, out_ref, x):
        gain = gain_ref[...].reshape(1, width)
        put_rows(x, 0, own_ref[...].astype(f32))
        for j in range(4):
            rows, inverse = normalize(every_fourth(x, j, patches // 4))
            upstream = mine_ref[j] + theirs_ref[j].astype(f32)
            result = grad_ref[j].astype(f32) + normalize_back(
                upstream, rows, inverse, gain
            )
            for c in range(x.shape[0]):
                x[c, pl.ds(j, patches // 4, stride=4), :] = result[:, c * LANES : (c + 1) * LANES]
        out_ref[...] = jnp.concatenate([x[c] for c in range(x.shape[0])], axis=1).astype(bf16)

    operands = (own, gain, mine, theirs, out_grad)
    return run_kernel(
        body,
        (1,),
        [whole(x) for x in operands],
        pl.BlockSpec((patches, width), lambda i, *_: (0, 0)),
        struct((patches, width), bf16),
        [pltpu.VMEM((width // LANES, patches, LANES), f32)],
    )(*operands)


def local_paired(
    grad_llm,
    vis_slot,
    image_rows,
    section_layer,
    vit_in,
    vit_out,
    ln_gain,
    ln_bias,
    qkv_weight,
    proj_weight,
    merge_gain,
    merge_bias,
    fc1_weight,
    fc1_bias,
    fc2_weight,
):
    sections = lax.axis_size("section")
    shards = lax.axis_size("vit")
    copies = lax.axis_size("dp")
    section_index = lax.axis_index("section")
    llm_width = grad_llm.shape[2]
    vit_width = vit_in.shape[1]
    head_dim = vit_width // HEADS
    group_rows = grad_llm.shape[1] // sections
    image_rows = image_rows.T

    outgoing = grad_llm[0].reshape(sections, group_rows, llm_width)
    arrived = {
        k: swap(
            lax.dynamic_index_in_dim(outgoing, section_index ^ k, 0, keepdims=False), "section", k
        )
        for k in range(1, sections)
    }
    vit_out_other = swap(vit_out, "vit", 1)
    piece, *own_parts = own_columns(qkv_weight, proj_weight, shards, copies)
    near = swap(piece, "section", 1)
    far = swap(piece, "section", 2)
    vit_in_other = swap(vit_in, "vit", 1)
    slope = slope_of(vit_out, vit_out_other, merge_gain, merge_bias, fc1_weight, fc1_bias)
    arrived, slope = lax.optimization_barrier((arrived, slope))

    summed = weighted_sum(section_layer, grad_llm, [arrived[k] for k in range(1, sections)])
    summed_other = swap(summed, "vit", 1)
    near, summed_other = lax.optimization_barrier((near, summed_other))
    near_chip = swap(near, "dp", 2)
    near_core = swap(near, "dp", 1)

    pre_grad = pre_grad_of(image_rows, vis_slot, summed, summed_other, fc2_weight, slope)
    far, near_chip, pre_grad = lax.optimization_barrier((far, near_chip, pre_grad))
    cross = swap(far, "section", 1)
    far_chip = swap(far, "dp", 2)
    near_diagonal = swap(near_chip, "dp", 1)
    far_core = swap(far, "dp", 1)
    first = merge_part(pre_grad, fc1_weight, 0, 2)
    first_theirs = swap(first, "vit", 1)
    second = merge_part(pre_grad, fc1_weight, 1, 2)
    second, cross, far_chip = lax.optimization_barrier((second, cross, far_chip))
    columns = own_parts[1].shape[1]
    cross_chip = swap(cross[:, :columns], "dp", 2)
    late_proj = swap(far_chip[:, columns:], "section", 1)
    second_theirs = swap(second, "vit", 1)
    cross_core = swap(cross, "dp", 1)
    far_diagonal = swap(far_chip, "dp", 1)
    sums, last_rows = project_early(
        vit_in,
        vit_in_other,
        ln_gain,
        ln_bias,
        [
            own_parts,
            [near, near_core, near_chip, near_diagonal],
            [far, far_core, far_chip, far_diagonal],
        ],
        sections,
    )
    cross_chip, late_proj, sums = lax.optimization_barrier((cross_chip, late_proj, sums))
    cross_diagonal = swap(cross_chip, "dp", 1)
    late_proj_core = swap(late_proj, "dp", 1)
    weights = [
        own_parts,
        [near, near_core, near_chip, near_diagonal],
        [far, far_core, far_chip, far_diagonal],
        [cross, cross_core, cross_chip, cross_diagonal],
    ]
    proj_apart = {(3, 2): late_proj, (3, 3): late_proj_core}

    projected = project_late(sums, last_rows, weights[-1], head_dim)
    normed_mine, normed_sent, out_grad = attention_back(
        image_rows,
        vit_out,
        vit_out_other,
        merge_gain,
        [first, second],
        [first_theirs, second_theirs],
        proj_weight,
        proj_apart,
        projected,
        weights,
        head_dim,
    )
    normed_theirs = swap(normed_sent, "vit", 1)
    return finish(vit_in, ln_gain, normed_mine, normed_theirs, out_grad)


def solution(mesh):
    paired = fits(mesh)

    def chosen_form(*arguments):
        return (local_paired if paired else local)(*arguments)

    placed = (
        P("section", ("dp", "vit"), None),
        P("dp", None),
        P("dp", None),
        P(),
        P(("dp", "section", "vit"), None),
        P(("dp", "section", "vit"), None),
        P(),
        P(),
        P("section", None),
        P("section", None),
        P(),
        P(),
        P(None, "vit"),
        P("vit"),
        P("vit", None),
    )
    return jax.shard_map(
        chosen_form,
        mesh=mesh,
        in_specs=placed,
        out_specs=P(("dp", "section", "vit"), None),
        check_vma=False,
    )
```
